1024 devices in a mesh: seq: 128 (over x, z, core), chan: 8 (over y).
Axes of the slice: x: 4, y: 8, z: 16, core: 2. Of those that a mesh axis runs over, the one named last changes fastest.
Arguments:
- grad_out: bfloat16 [16384, 4096], P('seq', 'chan'), may hold values from -30 to 30
- gate_query: bfloat16 [16384, 4096], P('seq', 'chan'), may hold values from -5 to 5
- key_input: bfloat16 [16384, 4096], P('seq', 'chan'), may hold values from -5 to 5
- value_input: bfloat16 [16384, 4096], P('seq', 'chan'), may hold values from -5 to 5
- decay_rate: float32 [16, 4096], P(None, 'chan'), as said below
- pole_angle: float32 [16, 4096], P(None, 'chan'), may hold values from 0.2 to 3
- residue: float32 [2, 16, 4096], P(None, None, 'chan'), may hold values from -3 to 3
- skip_gain: float32 [4096], P('chan'), may hold values from -4 to 4
Outputs:
- grad_key: bfloat16 [16384, 4096], P('seq', 'chan')
- grad_value: bfloat16 [16384, 4096], P('seq', 'chan')
- grad_residue: float32 [2, 16, 4096], P(None, None, 'chan')
The draws below stay inside these ranges and needn't reach their ends.
Inputs may be any that keep to these rules, and one draw needn't show every extreme that they name: `decay_rate`: each rate lies between 0.5 / 16384 and 1 / 30.
All inputs are finite; a program needn't handle non-finite values.
Results may differ from the reference program's by a relative error of at most 0.0049.
Values sent between devices are 32-bit elements; how exact they have to be, the bound alone decides.
No kernel may reach another device: no remote copies, remote signals or barrier semaphores. Data moves between devices by JAX's collectives and lax.ppermute only.
A program may use at most 64 MiB of HBM per device.

```python
import jax
import jax.numpy as jnp
from jax import lax

D = 4096
MODES = 16
SEQ_LEN = 16384


def draw_grad_out(key, part):
    noise_key = jax.random.fold_in(key, 0)
    channel = jnp.arange(D, dtype=jnp.float32)
    rising = jnp.exp(jnp.log(10.0) * (channel / D - 0.5))
    drawn_values = jnp.clip(jax.random.normal(noise_key, (SEQ_LEN, D), jnp.float32), -4.0, 4.0) * rising
    return drawn_values.astype(jnp.bfloat16)


def draw_decay_rate(key, part):
    slow_key = jax.random.fold_in(key, 1)
    lowest = jnp.log(0.5 / SEQ_LEN)
    drawn_rates = jnp.exp(jax.random.uniform(slow_key, (MODES, D), jnp.float32, lowest, jnp.log(1.0 / 30.0)))
    return drawn_rates.astype(jnp.float32)


def block_scale(key, shape, pieces, low, high):
    loudness, own = 1.0, jax.random.fold_in(key, 6)
    for position, shards_of in pieces:
        heights = jnp.exp(jax.random.uniform(jax.random.fold_in(own, position), (shards_of,), jnp.float32, low / len(pieces), high / len(pieces)))
        loudness = loudness * jnp.repeat(heights, shape[position] // shards_of).reshape([-1 if axis == position else 1 for axis in range(len(shape))])
    return loudness


def normal_values(rng, dims, scale, most, shards=(), held_as=jnp.bfloat16):
    result = scale * jax.random.normal(rng, dims, jnp.float32)
    if shards:
        result = result * block_scale(rng, dims, shards, -0.22, 0.18)
    return jnp.clip(result, -most, most).astype(held_as)


def setup_inputs(seed: int = 0) -> dict:
    key_of = jax.random.split(jax.random.key(seed), 9)
    grad_out = draw_grad_out(jax.random.fold_in(key_of[8], 71), 0)
    gate_query = normal_values(key_of[1], (SEQ_LEN, D), 1.0, 5.0, ((0, 128), (1, 8)))
    key_input = normal_values(key_of[2], (SEQ_LEN, D), 1.0, 5.0, ((0, 128), (1, 8)))
    value_input = normal_values(key_of[3], (SEQ_LEN, D), 1.0, 5.0, ((0, 128), (1, 8)))
    decay_rate = draw_decay_rate(jax.random.fold_in(key_of[8], 71), 0)
    pole_angle = jnp.clip(0.2 + 2.8 * jax.random.uniform(key_of[5], (MODES, D), jnp.float32) ** block_scale(key_of[5], (MODES, D), ((1, 8),), -0.2, 0.2), 0.2, 3.0)
    residue = normal_values(key_of[6], (2, MODES, D), 0.5, 3.0, ((2, 8),), jnp.float32)
    skip_gain = normal_values(key_of[7], (D,), 1.0, 4.0, ((0, 8),), jnp.float32)
    return dict(grad_out=grad_out, gate_query=gate_query, key_input=key_input, value_input=value_input, decay_rate=decay_rate, pole_angle=pole_angle, residue=residue, skip_gain=skip_gain)


def modal_block(inputs):
    grad_block, query_block, key_block, value_block, decay_block, angle_block, residue_block, skip_block = inputs
    weighted = grad_block.astype(jnp.float32) * query_block.astype(jnp.float32)
    key_values = key_block.astype(jnp.float32)
    value_values = value_block.astype(jnp.float32)
    stored = key_values * value_values
    norm_scale = jnp.sqrt(1.0 - jnp.exp(-2.0 * decay_block))
    residue_real = residue_block[0] * norm_scale
    residue_imaginary = residue_block[1] * norm_scale
    radius = jnp.exp(-decay_block)
    step_real = radius * jnp.cos(angle_block)
    step_imaginary = -radius * jnp.sin(angle_block)

    def advance(state, row_inputs):
        prior_real, prior_imaginary, total_real, total_imaginary = state
        weight_row, stored_row = row_inputs
        next_real = weight_row + step_real * prior_real - step_imaginary * prior_imaginary
        next_imaginary = step_real * prior_imaginary + step_imaginary * prior_real
        signal = lax.optimization_barrier(jnp.sum(residue_real * next_real - residue_imaginary * next_imaginary, axis=0))
        return ((next_real, next_imaginary, total_real + stored_row * next_real, total_imaginary + stored_row * next_imaginary), signal)
    zero_state = jnp.zeros(decay_block.shape, jnp.float32)
    final_state, modal = lax.scan(advance, (zero_state, zero_state, zero_state, zero_state), (weighted, stored), reverse=True)
    grad_signal = modal + skip_block * weighted
    grad_key = (grad_signal * value_values).astype(jnp.bfloat16)
    grad_value = (grad_signal * key_values).astype(jnp.bfloat16)
    raw_residue = jnp.stack([norm_scale * final_state[2], -norm_scale * final_state[3]])
    return (grad_key, grad_value, raw_residue)

def reference(grad_out, gate_query, key_input, value_input, decay_rate, pole_angle, residue, skip_gain):
    block_width = min(D, 1024)
    block_count = D // block_width

    def by_block(array):
        return array.reshape(array.shape[0], block_count, block_width).transpose(1, 0, 2)
    residue_blocks = residue.reshape(2, MODES, block_count, block_width).transpose(2, 0, 1, 3)
    skip_blocks = skip_gain.reshape(block_count, block_width)
    key_blocks, value_blocks, raw_blocks = lax.map(modal_block, (by_block(grad_out), by_block(gate_query), by_block(key_input), by_block(value_input), by_block(decay_rate), by_block(pole_angle), residue_blocks, skip_blocks))
    grad_key = key_blocks.transpose(1, 0, 2).reshape(SEQ_LEN, D)
    grad_value = value_blocks.transpose(1, 0, 2).reshape(SEQ_LEN, D)
    raw_residue = raw_blocks.transpose(1, 2, 0, 3).reshape(2, MODES, D)
    residue_norm = jnp.sqrt(jnp.sum(raw_residue * raw_residue))
    clip_level = jnp.sqrt(jnp.float32(2 * MODES * D))
    grad_residue = raw_residue * (clip_level / jnp.maximum(residue_norm, clip_level))
    return (grad_key, grad_value, grad_residue)
```

```python
import functools
import math

import jax
import jax.numpy as jnp
from jax import lax
from jax.experimental import pallas as pl
from jax.experimental.pallas import tpu as pltpu
from jax.sharding import PartitionSpec as P

LANES = 128
HALF = 64
SUB = 8
TURN_PARTS = (1.5703125, 4.837512969970703e-4, 7.54978995489188e-8)


def sine_cosine(angle):
    quarter = jnp.floor(angle * (2.0 / math.pi) + 0.5)
    rest = angle
    for part in TURN_PARTS:
        rest = rest - quarter * part
    square = rest * rest
    sine = ((-1.9515295891e-4 * square + 8.3321608736e-3) * square - 1.6666654611e-1) * square * rest + rest
    cosine = ((2.443315711809948e-5 * square - 1.388731625493765e-3) * square + 4.166664568298827e-2) * square * square
    cosine = cosine - 0.5 * square + 1.0
    index = quarter - 4.0 * jnp.floor(quarter * 0.25)
    odd = (index == 1.0) | (index == 3.0)
    sine_out = jnp.where(odd, cosine, sine)
    cosine_out = jnp.where(odd, sine, cosine)
    sine_out = jnp.where(index >= 2.0, -sine_out, sine_out)
    cosine_out = jnp.where((index == 1.0) | (index == 2.0), -cosine_out, cosine_out)
    return sine_out, cosine_out


def scale_of(decay):
    twice = 2.0 * decay
    series = 1.0 - twice * (1.0 / 7.0)
    for divisor in (6.0, 5.0, 4.0, 3.0, 2.0):
        series = 1.0 - twice * (1.0 / divisor) * series
    return jnp.sqrt(jnp.where(twice < 0.25, twice * series, 1.0 - jnp.exp(-twice)))


def spread(ref, row, columns=slice(None)):
    return jnp.broadcast_to(ref[pl.ds(row, 1), columns], (SUB, ref[pl.ds(row, 1), columns].shape[1]))


def lane_low(shape):
    return lax.broadcasted_iota(jnp.int32, shape, 1) < HALF


def pack_slices(real, imaginary, store):
    modes, width = real.shape
    low = lane_low((modes, LANES))
    for tile in range(width // LANES):
        re = real[:, tile * LANES : (tile + 1) * LANES]
        im = imaginary[:, tile * LANES : (tile + 1) * LANES]
        store(2 * tile * modes, jnp.where(low, re, pltpu.roll(im, HALF, 1)))
        store((2 * tile + 1) * modes, jnp.where(low, pltpu.roll(re, HALF, 1), im))


def unpack_slices(load, modes, width):
    low = lane_low((modes, LANES))
    reals, imaginaries = [], []
    for tile in range(width // LANES):
        even, odd = load(2 * tile * modes), load((2 * tile + 1) * modes)
        reals.append(jnp.where(low, even, pltpu.roll(odd, HALF, 1)))
        imaginaries.append(jnp.where(low, pltpu.roll(even, HALF, 1), odd))
    return jnp.concatenate(reals, axis=1), jnp.concatenate(imaginaries, axis=1)


def local_kernel(grad_ref, gate_ref, key_ref, value_ref, decay_ref, angle_ref, packed_ref, power_ref, weighted, stored):
    rows = grad_ref.shape[0]
    modes, width = decay_ref.shape
    weighted[...] = grad_ref[...].astype(jnp.float32) * gate_ref[...].astype(jnp.float32)
    stored[...] = key_ref[...].astype(jnp.float32) * value_ref[...].astype(jnp.float32)
    decay, angle = decay_ref[...], angle_ref[...]
    sine, cosine = sine_cosine(angle)
    radius = jnp.exp(-decay)
    step_real, step_imaginary = radius * cosine, -radius * sine
    span_sine, span_cosine = sine_cosine(angle * float(rows))
    span_radius = jnp.exp(-decay * float(rows))
    power_real, power_imaginary = span_radius * span_cosine, -span_radius * span_sine

    def store_power(column):
        def store(row, value):
            power_ref[row : row + modes, column : column + LANES] = value

        return store

    pack_slices(power_real, power_real, store_power(0))
    pack_slices(-power_imaginary, power_imaginary, store_power(LANES))
    parts = [[] for _ in range(6)]
    for first in range(0, modes, SUB):
        sr, si = step_real[first : first + SUB], step_imaginary[first : first + SUB]

        def block(j, carry, sr=sr, si=si):
            br, bi, lr, li, kr, ki = carry
            for r in range(SUB):
                t = rows - 1 - (j * SUB + r)
                w, s, s_up = spread(weighted, t), spread(stored, t), spread(stored, j * SUB + r)
                br, bi = (w + sr * br) - si * bi, sr * bi + si * br
                lr, li = lr + s * br, li + s * bi
                kr = kr + s_up
                kr, ki = sr * kr - si * ki, sr * ki + si * kr
            return br, bi, lr, li, kr, ki

        zero = jnp.zeros((SUB, width), jnp.float32)
        done = lax.fori_loop(0, rows // SUB, block, (zero,) * 6)
        for part, value in zip(parts, done):
            part.append(value)
    whole = [jnp.concatenate(part, axis=0) for part in parts]
    for which in range(3):

        def store(row, value, column=which * LANES):
            packed_ref[row : row + modes, column : column + LANES] = value

        pack_slices(whole[2 * which], whole[2 * which + 1], store)


def times(first, second_direct, second_cross):
    return first * second_direct + pltpu.roll(first, HALF, 1) * second_cross


def scan_kernel(where_ref, packed_ref, power_ref, out_ref):
    rows = packed_ref.shape[0]
    low = lane_low((1, LANES))
    mine = lax.broadcasted_iota(jnp.int32, power_ref.shape, 0) == where_ref[0]
    power = jnp.sum(jnp.where(mine, power_ref[...], 0.0), axis=0, keepdims=True)
    direct, cross = power[:, 0:LANES], power[:, LANES : 2 * LANES]
    state = packed_ref[:, 0:LANES]
    index = lax.broadcasted_iota(jnp.int32, (rows, LANES), 0)

    def from_later(value, shift):
        return jnp.where(index < rows - shift, pltpu.roll(value, rows - shift, 0), 0.0)

    state = from_later(state, 1)
    shift = 1
    while shift < rows:
        state = state + times(from_later(state, shift), direct, cross)
        real = jnp.where(low, direct, pltpu.roll(direct, HALF, 1))
        direct, cross = real * real - cross * cross, 2.0 * real * cross
        shift *= 2
    sums = packed_ref[:, LANES : 2 * LANES]
    reach = packed_ref[:, 2 * LANES : 3 * LANES]
    swapped = pltpu.roll(reach, HALF, 1)
    low_rows = lane_low((rows, LANES))
    reach_direct = jnp.where(low_rows, reach, swapped)
    reach_cross = jnp.where(low_rows, -swapped, reach)
    total = jnp.sum(sums + times(state, reach_direct, reach_cross), axis=0, keepdims=True)
    out_ref[:, 0:LANES] = state
    out_ref[:, LANES : 2 * LANES] = jnp.broadcast_to(total, (rows, LANES))


def residue_kernel(back_ref, decay_ref, raw_ref, squares_ref):
    modes, width = decay_ref.shape
    scale = scale_of(decay_ref[...])
    real, imaginary = unpack_slices(lambda row: back_ref[row : row + modes, LANES : 2 * LANES], modes, width)
    real, imaginary = real * scale, -(imaginary * scale)
    raw_ref[0] = real
    raw_ref[1] = imaginary
    squares = jnp.sum(real * real + imaginary * imaginary, axis=0, keepdims=True)
    total = squares[:, 0:LANES]
    for tile in range(1, width // LANES):
        total = total + squares[:, tile * LANES : (tile + 1) * LANES]
    squares_ref[...] = jnp.broadcast_to(total, squares_ref.shape)


def signal_kernel(
    back_ref, grad_ref, gate_ref, key_ref, value_ref, decay_ref, angle_ref, residue_ref, skip_ref,
    grad_key_ref, grad_value_ref, weighted, signal,
):
    rows = grad_ref.shape[0]
    modes, width = decay_ref.shape
    weighted[...] = grad_ref[...].astype(jnp.float32) * gate_ref[...].astype(jnp.float32)
    decay = decay_ref[...]
    sine, cosine = sine_cosine(angle_ref[...])
    radius = jnp.exp(-decay)
    step_real, step_imaginary = radius * cosine, -radius * sine
    scale = scale_of(decay)
    weight_real, weight_imaginary = residue_ref[0] * scale, residue_ref[1] * scale
    real, imaginary = unpack_slices(lambda row: back_ref[row : row + modes, 0:LANES], modes, width)
    start_real = weight_real * real - weight_imaginary * imaginary
    start_imaginary = weight_real * imaginary + weight_imaginary * real
    span = 2 * LANES
    for column in range(0, width, span):
        cut = slice(column, column + span)
        steps = [
            tuple(a[first : first + SUB, cut] for a in (step_real, step_imaginary, weight_real, weight_imaginary))
            for first in range(0, modes, SUB)
        ]
        begin = tuple(
            a[first : first + SUB, cut] for first in range(0, modes, SUB) for a in (start_real, start_imaginary)
        )

        def block(j, carry, steps=steps, cut=cut):
            carry = list(carry)
            for r in range(SUB):
                t = rows - 1 - (j * SUB + r)
                w = spread(weighted, t, cut)
                total = None
                for which, (sr, si, cr, ci) in enumerate(steps):
                    qr, qi = carry[2 * which], carry[2 * which + 1]
                    qr, qi = (cr * w + sr * qr) - si * qi, (ci * w + sr * qi) + si * qr
                    carry[2 * which], carry[2 * which + 1] = qr, qi
                    total = qr if total is None else total + qr
                place = pl.ds(pl.multiple_of(t * SUB, SUB), SUB)
                for part in range(span // LANES):
                    view = signal.at[cut.start // LANES + part]
                    view[place, :] = total[:, part * LANES : (part + 1) * LANES]
            return tuple(carry)

        lax.fori_loop(0, rows // SUB, block, begin)
    summed = skip_ref[...] * weighted[...]
    for tile in range(width // LANES):
        cut = slice(tile * LANES, (tile + 1) * LANES)
        part = summed[:, cut]
        view = signal.at[tile]
        for member in range(SUB):
            part = part + view[pl.ds(member, rows, stride=SUB), :]
        grad_key_ref[:, cut] = (part * value_ref[:, cut].astype(jnp.float32)).astype(jnp.bfloat16)
        grad_value_ref[:, cut] = (part * key_ref[:, cut].astype(jnp.float32)).astype(jnp.bfloat16)


def clip_kernel(clip_level, squares_ref, raw_ref, out_ref):
    norm = jnp.sqrt(jnp.sum(squares_ref[...], keepdims=True))
    out_ref[...] = raw_ref[...] * (clip_level / jnp.maximum(norm, clip_level))[None]


def on_device(
    grad_out, gate_query, key_input, value_input, decay_rate, pole_angle, residue, skip_gain
):
    rows, width = grad_out.shape
    modes = decay_rate.shape[0]
    shards, chan_shards = lax.axis_size("seq"), lax.axis_size("chan")
    slices = modes * width // HALF
    packed, power = pl.pallas_call(
        local_kernel,
        out_shape=(
            jax.ShapeDtypeStruct((slices, 3 * LANES), jnp.float32),
            jax.ShapeDtypeStruct((slices, 2 * LANES), jnp.float32),
        ),
        scratch_shapes=[pltpu.VMEM((rows, width), jnp.float32)] * 2,
        name="local_pass",
    )(grad_out, gate_query, key_input, value_input, decay_rate, pole_angle)
    turned = lax.all_to_all(packed, "seq", 0, 0, tiled=True)
    where = lax.axis_index("seq").reshape(1)
    answers = pl.pallas_call(
        scan_kernel,
        in_specs=[pl.BlockSpec(memory_space=pltpu.SMEM)] + [pl.BlockSpec(memory_space=pltpu.VMEM)] * 2,
        out_shape=jax.ShapeDtypeStruct((shards, 2 * LANES), jnp.float32),
        name="scan_shards",
    )(where, turned, power)
    back = lax.all_to_all(answers, "seq", 0, 0, tiled=True)
    raw, squares = pl.pallas_call(
        residue_kernel,
        out_shape=(
            jax.ShapeDtypeStruct((2, modes, width), jnp.float32),
            jax.ShapeDtypeStruct((chan_shards, LANES), jnp.float32),
        ),
        name="residue_sums",
    )(back, decay_rate)
    all_squares = lax.all_to_all(squares, "chan", 0, 0, tiled=True)
    grad_key, grad_value = pl.pallas_call(
        signal_kernel,
        out_shape=(jax.ShapeDtypeStruct((rows, width), jnp.bfloat16),) * 2,
        scratch_shapes=[
            pltpu.VMEM((rows, width), jnp.float32),
            pltpu.VMEM((width // LANES, rows * SUB, LANES), jnp.float32),
        ],
        cost_estimate=pl.CostEstimate(flops=20 * rows * width * modes, bytes_accessed=12 * rows * width, transcendentals=0),
        name="signal_pass",
    )(back, grad_out, gate_query, key_input, value_input, decay_rate, pole_angle, residue, skip_gain.reshape(1, width))
    clip_level = math.sqrt(2 * modes * width * chan_shards)
    grad_residue = pl.pallas_call(
        functools.partial(clip_kernel, clip_level),
        out_shape=jax.ShapeDtypeStruct((2, modes, width), jnp.float32),
        name="clip",
    )(all_squares, raw)
    return (grad_key, grad_value, grad_residue)


def solution(mesh):
    return jax.shard_map(
        on_device,
        mesh=mesh,
        in_specs=(
            P("seq", "chan"),
            P("seq", "chan"),
            P("seq", "chan"),
            P("seq", "chan"),
            P(None, "chan"),
            P(None, "chan"),
            P(None, None, "chan"),
            P("chan"),
        ),
        out_specs=(P("seq", "chan"), P("seq", "chan"), P(None, None, "chan")),
        check_vma=False,
    )
```

```python
import functools
import math

import jax
import jax.numpy as jnp
from jax import lax
from jax.experimental import pallas as pl
from jax.experimental.pallas import tpu as pltpu
from jax.sharding import PartitionSpec as P

LANES = 128
HALF = 64
SUB = 8
TURN_PARTS = (1.5703125, 4.837512969970703e-4, 7.54978995489188e-8)


def sine_cosine(angle):
    quarter = jnp.floor(angle * (2.0 / math.pi) + 0.5)
    rest = angle
    for part in TURN_PARTS:
        rest = rest - quarter * part
    square = rest * rest
    sine = ((-1.9515295891e-4 * square + 8.3321608736e-3) * square - 1.6666654611e-1) * square * rest + rest
    cosine = ((2.443315711809948e-5 * square - 1.388731625493765e-3) * square + 4.166664568298827e-2) * square * square
    cosine = cosine - 0.5 * square + 1.0
    index = quarter - 4.0 * jnp.floor(quarter * 0.25)
    odd = (index == 1.0) | (index == 3.0)
    sine_out = jnp.where(odd, cosine, sine)
    cosine_out = jnp.where(odd, sine, cosine)
    sine_out = jnp.where(index >= 2.0, -sine_out, sine_out)
    cosine_out = jnp.where((index == 1.0) | (index == 2.0), -cosine_out, cosine_out)
    return sine_out, cosine_out


def scale_of(decay):
    twice = 2.0 * decay
    series = 1.0 - twice * (1.0 / 7.0)
    for divisor in (6.0, 5.0, 4.0, 3.0, 2.0):
        series = 1.0 - twice * (1.0 / divisor) * series
    return jnp.sqrt(jnp.where(twice < 0.25, twice * series, 1.0 - jnp.exp(-twice)))


def line_block(ref, first, columns=slice(None)):
    block = ref[pl.ds(pl.multiple_of(first, SUB), SUB), columns]
    return [jnp.broadcast_to(block[r : r + 1], block.shape) for r in range(SUB)]


def lane_low(shape):
    return lax.broadcasted_iota(jnp.int32, shape, 1) < HALF


def pack_slices(real, imaginary, store):
    modes, width = real.shape
    low = lane_low((modes, LANES))
    for tile in range(width // LANES):
        re = real[:, tile * LANES : (tile + 1) * LANES]
        im = imaginary[:, tile * LANES : (tile + 1) * LANES]
        store(2 * tile * modes, jnp.where(low, re, pltpu.roll(im, HALF, 1)))
        store((2 * tile + 1) * modes, jnp.where(low, pltpu.roll(re, HALF, 1), im))


def unpack_slices(load, modes, width):
    low = lane_low((modes, LANES))
    reals, imaginaries = [], []
    for tile in range(width // LANES):
        even, odd = load(2 * tile * modes), load((2 * tile + 1) * modes)
        reals.append(jnp.where(low, even, pltpu.roll(odd, HALF, 1)))
        imaginaries.append(jnp.where(low, pltpu.roll(even, HALF, 1), odd))
    return jnp.concatenate(reals, axis=1), jnp.concatenate(imaginaries, axis=1)


def local_kernel(grad_ref, gate_ref, key_ref, value_ref, decay_ref, angle_ref, packed_ref, weighted, stored):
    rows = grad_ref.shape[0]
    modes, width = decay_ref.shape
    weighted[...] = grad_ref[...].astype(jnp.float32) * gate_ref[...].astype(jnp.float32)
    stored[...] = key_ref[...].astype(jnp.float32) * value_ref[...].astype(jnp.float32)
    decay, angle = decay_ref[...], angle_ref[...]
    sine, cosine = sine_cosine(angle)
    radius = jnp.exp(-decay)
    step_real, step_imaginary = radius * cosine, -radius * sine
    parts = [[] for _ in range(6)]
    for first in range(0, modes, SUB):
        sr, si = step_real[first : first + SUB], step_imaginary[first : first + SUB]

        def block(j, carry, sr=sr, si=si):
            br, bi, lr, li, kr, ki = carry
            last = rows - SUB - j * SUB
            ws, ss, ups = line_block(weighted, last), line_block(stored, last), line_block(stored, j * SUB)
            for r in range(SUB):
                w, s, s_up = ws[SUB - 1 - r], ss[SUB - 1 - r], ups[r]
                br, bi = (w + sr * br) - si * bi, sr * bi + si * br
                lr, li = lr + s * br, li + s * bi
                kr = kr + s_up
                kr, ki = sr * kr - si * ki, sr * ki + si * kr
            return br, bi, lr, li, kr, ki

        zero = jnp.zeros((SUB, width), jnp.float32)
        done = lax.fori_loop(0, rows // SUB, block, (zero,) * 6)
        for part, value in zip(parts, done):
            part.append(value)
    whole = [jnp.concatenate(part, axis=0) for part in parts]
    for which in range(3):

        def store(row, value, which=which):
            packed_ref[pl.ds(3 * row + which, modes, stride=3), :] = value

        pack_slices(whole[2 * which], whole[2 * which + 1], store)


def times(first, second_direct, second_cross):
    return first * second_direct + pltpu.roll(first, HALF, 1) * second_cross


def slice_values(ref, where):
    modes, width = ref.shape
    mode, block = lax.rem(where, modes), lax.div(where, modes)
    chosen = jnp.zeros((modes, LANES), jnp.float32)
    for tile in range(width // LANES):
        chosen = jnp.where(lax.div(block, 2) == tile, ref[:, tile * LANES : (tile + 1) * LANES], chosen)
    rows = lax.broadcasted_iota(jnp.int32, chosen.shape, 0)
    line = jnp.sum(jnp.where(rows == mode, chosen, 0.0), axis=0, keepdims=True)
    line = jnp.where(lane_low(line.shape) == (lax.rem(block, 2) == 0), line, 0.0)
    return line + pltpu.roll(line, HALF, 1)


def scan_kernel(span, where_ref, packed_ref, decay_ref, angle_ref, out_ref):
    rows = packed_ref.shape[0] // 3
    low = lane_low((1, LANES))
    decay, angle = slice_values(decay_ref, where_ref[0]), slice_values(angle_ref, where_ref[0])
    sine, cosine = sine_cosine(angle * float(span))
    radius = jnp.exp(-decay * float(span))
    direct, cross = radius * cosine, jnp.where(low, radius * sine, -radius * sine)
    state = packed_ref[pl.ds(0, rows, stride=3), :]
    index = lax.broadcasted_iota(jnp.int32, (rows, LANES), 0)

    def from_later(value, shift):
        return jnp.where(index < rows - shift, pltpu.roll(value, rows - shift, 0), 0.0)

    state = from_later(state, 1)
    shift = 1
    while shift < rows:
        state = state + times(from_later(state, shift), direct, cross)
        direct, cross = direct * direct - cross * cross, 2.0 * direct * cross
        shift *= 2
    sums = packed_ref[pl.ds(1, rows, stride=3), :]
    reach = packed_ref[pl.ds(2, rows, stride=3), :]
    swapped = pltpu.roll(reach, HALF, 1)
    low_rows = lane_low((rows, LANES))
    reach_direct = jnp.where(low_rows, reach, swapped)
    reach_cross = jnp.where(low_rows, -swapped, reach)
    total = jnp.sum(sums + times(state, reach_direct, reach_cross), axis=0, keepdims=True)
    out_ref[pl.ds(0, rows, stride=2), :] = state
    out_ref[pl.ds(1, rows, stride=2), :] = jnp.broadcast_to(total, (rows, LANES))


def residue_kernel(back_ref, decay_ref, raw_ref, squares_ref):
    modes, width = decay_ref.shape
    scale = scale_of(decay_ref[...])
    real, imaginary = unpack_slices(lambda row: back_ref[pl.ds(2 * row + 1, modes, stride=2), :], modes, width)
    real, imaginary = real * scale, -(imaginary * scale)
    raw_ref[0] = real
    raw_ref[1] = imaginary
    squares = jnp.sum(real * real + imaginary * imaginary, axis=0, keepdims=True)
    total = squares[:, 0:LANES]
    for tile in range(1, width // LANES):
        total = total + squares[:, tile * LANES : (tile + 1) * LANES]
    squares_ref[...] = jnp.broadcast_to(total, squares_ref.shape)


def signal_kernel(
    back_ref, grad_ref, gate_ref, key_ref, value_ref, decay_ref, angle_ref, residue_ref, skip_ref,
    grad_key_ref, grad_value_ref, weighted, signal,
):
    rows = grad_ref.shape[0]
    modes, width = decay_ref.shape
    weighted[...] = grad_ref[...].astype(jnp.float32) * gate_ref[...].astype(jnp.float32)
    decay = decay_ref[...]
    sine, cosine = sine_cosine(angle_ref[...])
    radius = jnp.exp(-decay)
    step_real, step_imaginary = radius * cosine, -radius * sine
    scale = scale_of(decay)
    weight_real, weight_imaginary = residue_ref[0] * scale, residue_ref[1] * scale
    real, imaginary = unpack_slices(lambda row: back_ref[pl.ds(2 * row, modes, stride=2), :], modes, width)
    start_real = weight_real * real - weight_imaginary * imaginary
    start_imaginary = weight_real * imaginary + weight_imaginary * real
    span = 2 * LANES
    for column in range(0, width, span):
        cut = slice(column, column + span)
        steps = [
            tuple(a[first : first + SUB, cut] for a in (step_real, step_imaginary, weight_real, weight_imaginary))
            for first in range(0, modes, SUB)
        ]
        begin = tuple(
            a[first : first + SUB, cut] for first in range(0, modes, SUB) for a in (start_real, start_imaginary)
        )

        def block(j, carry, steps=steps, cut=cut):
            carry = list(carry)
            last = rows - SUB - j * SUB
            ws = line_block(weighted, last, cut)
            for r in range(SUB):
                t = last + SUB - 1 - r
                w = ws[SUB - 1 - r]
                total = None
                for which, (sr, si, cr, ci) in enumerate(steps):
                    qr, qi = carry[2 * which], carry[2 * which + 1]
                    qr, qi = (cr * w + sr * qr) - si * qi, (ci * w + sr * qi) + si * qr
                    carry[2 * which], carry[2 * which + 1] = qr, qi
                    total = qr if total is None else total + qr
                place = pl.ds(pl.multiple_of(t * SUB, SUB), SUB)
                for part in range(span // LANES):
                    view = signal.at[cut.start // LANES + part]
                    view[place, :] = total[:, part * LANES : (part + 1) * LANES]
            return tuple(carry)

        lax.fori_loop(0, rows // SUB, block, begin)
    summed = skip_ref[...] * weighted[...]
    for tile in range(width // LANES):
        cut = slice(tile * LANES, (tile + 1) * LANES)
        part = summed[:, cut]
        view = signal.at[tile]
        for member in range(SUB):
            part = part + view[pl.ds(member, rows, stride=SUB), :]
        grad_key_ref[:, cut] = (part * value_ref[:, cut].astype(jnp.float32)).astype(jnp.bfloat16)
        grad_value_ref[:, cut] = (part * key_ref[:, cut].astype(jnp.float32)).astype(jnp.bfloat16)


def clip_kernel(clip_level, squares_ref, raw_ref, out_ref):
    norm = jnp.sqrt(jnp.sum(squares_ref[...], keepdims=True))
    out_ref[...] = raw_ref[...] * (clip_level / jnp.maximum(norm, clip_level))[None]


def turn(array, parts):
    sent = array.reshape(array.shape[0] // parts, parts * LANES)
    return lax.all_to_all(sent, "seq", 0, 0, tiled=True).reshape(array.shape)


def on_device(
    grad_out, gate_query, key_input, value_input, decay_rate, pole_angle, residue, skip_gain
):
    rows, width = grad_out.shape
    modes = decay_rate.shape[0]
    shards, chan_shards = lax.axis_size("seq"), lax.axis_size("chan")
    slices = modes * width // HALF
    packed = pl.pallas_call(
        local_kernel,
        out_shape=jax.ShapeDtypeStruct((3 * slices, LANES), jnp.float32),
        scratch_shapes=[pltpu.VMEM((rows, width), jnp.float32)] * 2,
        name="local_pass",
    )(grad_out, gate_query, key_input, value_input, decay_rate, pole_angle)
    turned = turn(packed, 3)
    where = lax.axis_index("seq").reshape(1)
    answers = pl.pallas_call(
        functools.partial(scan_kernel, rows),
        in_specs=[pl.BlockSpec(memory_space=pltpu.SMEM)] + [pl.BlockSpec(memory_space=pltpu.VMEM)] * 3,
        out_shape=jax.ShapeDtypeStruct((2 * shards, LANES), jnp.float32),
        name="scan_shards",
    )(where, turned, decay_rate, pole_angle)
    back = turn(answers, 2)
    raw, squares = pl.pallas_call(
        residue_kernel,
        out_shape=(
            jax.ShapeDtypeStruct((2, modes, width), jnp.float32),
            jax.ShapeDtypeStruct((chan_shards, LANES), jnp.float32),
        ),
        name="residue_sums",
    )(back, decay_rate)
    all_squares = lax.all_to_all(squares, "chan", 0, 0, tiled=True)
    grad_key, grad_value = pl.pallas_call(
        signal_kernel,
        out_shape=(jax.ShapeDtypeStruct((rows, width), jnp.bfloat16),) * 2,
        scratch_shapes=[
            pltpu.VMEM((rows, width), jnp.float32),
            pltpu.VMEM((width // LANES, rows * SUB, LANES), jnp.float32),
        ],
        cost_estimate=pl.CostEstimate(flops=20 * rows * width * modes, bytes_accessed=12 * rows * width, transcendentals=0),
        name="signal_pass",
    )(back, grad_out, gate_query, key_input, value_input, decay_rate, pole_angle, residue, skip_gain.reshape(1, width))
    clip_level = math.sqrt(2 * modes * width * chan_shards)
    grad_residue = pl.pallas_call(
        functools.partial(clip_kernel, clip_level),
        out_shape=jax.ShapeDtypeStruct((2, modes, width), jnp.float32),
        name="clip",
    )(all_squares, raw)
    return (grad_key, grad_value, grad_residue)


def solution(mesh):
    return jax.shard_map(
        on_device,
        mesh=mesh,
        in_specs=(
            P("seq", "chan"),
            P("seq", "chan"),
            P("seq", "chan"),
            P("seq", "chan"),
            P(None, "chan"),
            P(None, "chan"),
            P(None, None, "chan"),
            P("chan"),
        ),
        out_specs=(P("seq", "chan"), P("seq", "chan"), P(None, None, "chan")),
        check_vma=False,
    )
```

```python
import functools
import math

import jax
import jax.numpy as jnp
from jax import lax
from jax.experimental import pallas as pl
from jax.experimental.pallas import tpu as pltpu
from jax.sharding import PartitionSpec as P

LANES = 128
HALF = 64
SUB = 8
CORES = 2
CHIPS_Z = 16
RUN = CORES * CHIPS_Z
TURN_PARTS = (1.5703125, 4.837512969970703e-4, 7.54978995489188e-8)


def sine_cosine(angle):
    quarter = jnp.floor(angle * (2.0 / math.pi) + 0.5)
    rest = angle
    for part in TURN_PARTS:
        rest = rest - quarter * part
    square = rest * rest
    sine = ((-1.9515295891e-4 * square + 8.3321608736e-3) * square - 1.6666654611e-1) * square * rest + rest
    cosine = ((2.443315711809948e-5 * square - 1.388731625493765e-3) * square + 4.166664568298827e-2) * square * square
    cosine = cosine - 0.5 * square + 1.0
    index = quarter - 4.0 * jnp.floor(quarter * 0.25)
    odd = (index == 1.0) | (index == 3.0)
    sine_out = jnp.where(odd, cosine, sine)
    cosine_out = jnp.where(odd, sine, cosine)
    sine_out = jnp.where(index >= 2.0, -sine_out, sine_out)
    cosine_out = jnp.where((index == 1.0) | (index == 2.0), -cosine_out, cosine_out)
    return sine_out, cosine_out


def scale_of(decay):
    twice = 2.0 * decay
    series = 1.0 - twice * (1.0 / 7.0)
    for divisor in (6.0, 5.0, 4.0, 3.0, 2.0):
        series = 1.0 - twice * (1.0 / divisor) * series
    return jnp.sqrt(jnp.where(twice < 0.25, twice * series, 1.0 - jnp.exp(-twice)))


def line_block(ref, first, columns=slice(None)):
    block = ref[pl.ds(pl.multiple_of(first, SUB), SUB), columns]
    return [jnp.broadcast_to(block[r : r + 1], block.shape) for r in range(SUB)]


def lane_low(shape):
    return lax.broadcasted_iota(jnp.int32, shape, 1) < HALF


def pack_slices(real, imaginary, store):
    low = lane_low((real.shape[0], LANES))
    for tile in range(real.shape[1] // LANES):
        re = real[:, tile * LANES : (tile + 1) * LANES]
        im = imaginary[:, tile * LANES : (tile + 1) * LANES]
        store(2 * tile, jnp.where(low, re, pltpu.roll(im, HALF, 1)))
        store(2 * tile + 1, jnp.where(low, pltpu.roll(re, HALF, 1), im))


def unpack_slices(load, modes, width):
    low = lane_low((modes, LANES))
    reals, imaginaries = [], []
    for tile in range(width // LANES):
        even, odd = load(2 * tile), load(2 * tile + 1)
        reals.append(jnp.where(low, even, pltpu.roll(odd, HALF, 1)))
        imaginaries.append(jnp.where(low, pltpu.roll(even, HALF, 1), odd))
    return jnp.concatenate(reals, axis=1), jnp.concatenate(imaginaries, axis=1)


def answer_lines(back_ref, part, modes):
    halves = modes // SUB

    def load(block):
        lines = [(block * halves + half) * 2 * SUB + part * SUB for half in range(halves)]
        return jnp.concatenate([back_ref[first : first + SUB] for first in lines], axis=0)

    return load


def local_kernel(grad_ref, gate_ref, key_ref, value_ref, decay_ref, angle_ref, packed_ref, weighted, stored):
    rows = grad_ref.shape[0]
    modes, width = decay_ref.shape
    weighted[...] = grad_ref[...].astype(jnp.float32) * gate_ref[...].astype(jnp.float32)
    stored[...] = key_ref[...].astype(jnp.float32) * value_ref[...].astype(jnp.float32)
    decay, angle = decay_ref[...], angle_ref[...]
    sine, cosine = sine_cosine(angle)
    radius = jnp.exp(-decay)
    step_real, step_imaginary = radius * cosine, -radius * sine
    for first in range(0, modes, SUB):
        sr, si = step_real[first : first + SUB], step_imaginary[first : first + SUB]

        def block(j, carry, sr=sr, si=si):
            br, bi, lr, li, kr, ki = carry
            last = rows - SUB - j * SUB
            ws, ss, ups = line_block(weighted, last), line_block(stored, last), line_block(stored, j * SUB)
            for r in range(SUB):
                w, s, s_up = ws[SUB - 1 - r], ss[SUB - 1 - r], ups[r]
                br, bi = (w + sr * br) - si * bi, sr * bi + si * br
                lr, li = lr + s * br, li + s * bi
                kr = kr + s_up
                kr, ki = sr * kr - si * ki, sr * ki + si * kr
            return br, bi, lr, li, kr, ki

        zero = jnp.zeros((SUB, width), jnp.float32)
        done = lax.fori_loop(0, rows // SUB, block, (zero,) * 6)
        for part in range(3):

            def store(block, value, part=part, half=first // SUB):
                line = (block * (modes // SUB) + half) * 3 * SUB + part * SUB
                packed_ref[line : line + SUB] = value

            pack_slices(done[2 * part], done[2 * part + 1], store)


def swap(value):
    return pltpu.roll(value, HALF, 1)


def factors(value, swapped):
    low = lane_low(value.shape)
    return jnp.where(low, value, swapped), jnp.where(low, -swapped, value)


def step(added, state, power):
    direct, cross = power
    here, there = state
    return added[0] + (here * direct + there * cross), added[1] + (there * direct - here * cross)


def squared(power):
    direct, cross = power
    return direct * direct - cross * cross, 2.0 * direct * cross


def place_of(where_ref):
    where = where_ref[0]
    return lax.div(where, RUN), lax.rem(lax.div(where, CORES), CHIPS_Z), lax.rem(where, CORES)


def slice_values(ref, chip):
    modes, width = ref.shape
    halves = modes // SUB
    block, half = lax.div(chip, halves), lax.rem(chip, halves)
    chosen = jnp.zeros((SUB, LANES), jnp.float32)
    for tile in range(width // LANES):
        for first in range(halves):
            here = (lax.div(block, 2) == tile) & (half == first)
            part = ref[first * SUB : (first + 1) * SUB, tile * LANES : (tile + 1) * LANES]
            chosen = jnp.where(here, part, chosen)
    chosen = jnp.where(lane_low(chosen.shape) == (lax.rem(block, 2) == 0), chosen, 0.0)
    return chosen + swap(chosen)


def span_power(span, decay_ref, angle_ref, chip):
    decay, angle = slice_values(decay_ref, chip), slice_values(angle_ref, chip)
    sine, cosine = sine_cosine(angle * float(span))
    radius = jnp.exp(-decay * float(span))
    return radius * cosine, jnp.where(lane_low(sine.shape), radius * sine, -radius * sine)


def run_kernel(span, where_ref, own_ref, other_ref, decay_ref, angle_ref, message_ref, inside_ref):
    _, chip, core = place_of(where_ref)
    power = span_power(span, decay_ref, angle_ref, chip)
    first_core = core == 0

    def tiles(part, z):
        line = (3 * z + part) * SUB
        own, other = own_ref[line : line + SUB], other_ref[line : line + SUB]
        pair = jnp.where(first_core, own, other), jnp.where(first_core, other, own)
        return [(value, swap(value)) for value in pair]

    zero = jnp.zeros((SUB, LANES), jnp.float32)
    state, total, reach = (zero, zero), zero, (zero, zero)
    for z in range(CHIPS_Z):
        for value in tiles(2, z):
            reach = step(value, reach, power)
    for z in reversed(range(CHIPS_Z)):
        carries, sums, reaches = tiles(0, z), tiles(1, z), tiles(2, z)
        inside = []
        for c in reversed(range(CORES)):
            inside.append(state[0])
            direct, cross = factors(*reaches[c])
            total = total + (sums[c][0] + (state[0] * direct + state[1] * cross))
            state = step(carries[c], state, power)
        inside_ref[z * SUB : (z + 1) * SUB] = jnp.where(first_core, inside[1], inside[0])
    copies = message_ref.shape[0] // (3 * SUB)
    for copy in range(copies):
        for part, value in enumerate((state[0], total, reach[0])):
            line = (3 * copy + part) * SUB
            message_ref[line : line + SUB] = value


def answer_kernel(span, where_ref, message_ref, inside_ref, decay_ref, angle_ref, out_ref):
    mine, chip, core = place_of(where_ref)
    power = span_power(span, decay_ref, angle_ref, chip)
    run_power = power
    for _ in range(RUN.bit_length() - 1):
        run_power = squared(run_power)
    zero = jnp.zeros((SUB, LANES), jnp.float32)
    state, total = (zero, zero), zero
    entering = (zero, zero)
    for x in reversed(range(message_ref.shape[0] // (3 * SUB))):
        carry, sums, reach = [message_ref[(3 * x + part) * SUB : (3 * x + part + 1) * SUB] for part in range(3)]
        entering = tuple(jnp.where(mine == x, new, old) for new, old in zip(state, entering))
        direct, cross = factors(reach, swap(reach))
        total = total + (sums + (state[0] * direct + state[1] * cross))
        state = step((carry, swap(carry)), state, run_power)
    moved = step((zero, zero), entering, power)
    entering = tuple(jnp.where(core == CORES - 1, here, there) for here, there in zip(entering, moved))
    chip_power = squared(power)
    for z in reversed(range(CHIPS_Z)):
        out_ref[2 * z * SUB : (2 * z + 1) * SUB] = inside_ref[z * SUB : (z + 1) * SUB] + entering[0]
        out_ref[(2 * z + 1) * SUB : (2 * z + 2) * SUB] = total
        entering = step((zero, zero), entering, chip_power)


def residue_kernel(back_ref, decay_ref, raw_ref, squares_ref):
    modes, width = decay_ref.shape
    scale = scale_of(decay_ref[...])
    real, imaginary = unpack_slices(answer_lines(back_ref, 1, modes), modes, width)
    real, imaginary = real * scale, -(imaginary * scale)
    raw_ref[0] = real
    raw_ref[1] = imaginary
    squares = jnp.sum(real * real + imaginary * imaginary, axis=0, keepdims=True)
    total = squares[:, 0:LANES]
    for tile in range(1, width // LANES):
        total = total + squares[:, tile * LANES : (tile + 1) * LANES]
    squares_ref[...] = jnp.broadcast_to(total, squares_ref.shape)


def signal_kernel(
    back_ref, grad_ref, gate_ref, key_ref, value_ref, decay_ref, angle_ref, residue_ref, skip_ref,
    grad_key_ref, grad_value_ref, weighted, signal,
):
    rows = grad_ref.shape[0]
    modes, width = decay_ref.shape
    weighted[...] = grad_ref[...].astype(jnp.float32) * gate_ref[...].astype(jnp.float32)
    decay = decay_ref[...]
    sine, cosine = sine_cosine(angle_ref[...])
    radius = jnp.exp(-decay)
    step_real, step_imaginary = radius * cosine, -radius * sine
    scale = scale_of(decay)
    weight_real, weight_imaginary = residue_ref[0] * scale, residue_ref[1] * scale
    real, imaginary = unpack_slices(answer_lines(back_ref, 0, modes), modes, width)
    start_real = weight_real * real - weight_imaginary * imaginary
    start_imaginary = weight_real * imaginary + weight_imaginary * real
    span = 2 * LANES
    for column in range(0, width, span):
        cut = slice(column, column + span)
        steps = [
            tuple(a[first : first + SUB, cut] for a in (step_real, step_imaginary, weight_real, weight_imaginary))
            for first in range(0, modes, SUB)
        ]
        begin = tuple(
            a[first : first + SUB, cut] for first in range(0, modes, SUB) for a in (start_real, start_imaginary)
        )

        def block(j, carry, steps=steps, cut=cut):
            carry = list(carry)
            last = rows - SUB - j * SUB
            ws = line_block(weighted, last, cut)
            for r in range(SUB):
                t = last + SUB - 1 - r
                w = ws[SUB - 1 - r]
                total = None
                for which, (sr, si, cr, ci) in enumerate(steps):
                    qr, qi = carry[2 * which], carry[2 * which + 1]
                    qr, qi = (cr * w + sr * qr) - si * qi, (ci * w + sr * qi) + si * qr
                    carry[2 * which], carry[2 * which + 1] = qr, qi
                    total = qr if total is None else total + qr
                place = pl.ds(pl.multiple_of(t * SUB, SUB), SUB)
                for part in range(span // LANES):
                    view = signal.at[cut.start // LANES + part]
                    view[place, :] = total[:, part * LANES : (part + 1) * LANES]
            return tuple(carry)

        lax.fori_loop(0, rows // SUB, block, begin)
    summed = skip_ref[...] * weighted[...]
    for tile in range(width // LANES):
        cut = slice(tile * LANES, (tile + 1) * LANES)
        part = summed[:, cut]
        view = signal.at[tile]
        for member in range(SUB):
            part = part + view[pl.ds(member, rows, stride=SUB), :]
        grad_key_ref[:, cut] = (part * value_ref[:, cut].astype(jnp.float32)).astype(jnp.bfloat16)
        grad_value_ref[:, cut] = (part * key_ref[:, cut].astype(jnp.float32)).astype(jnp.bfloat16)


def clip_kernel(clip_level, squares_ref, raw_ref, out_ref):
    norm = jnp.sqrt(jnp.sum(squares_ref[...], keepdims=True))
    out_ref[...] = raw_ref[...] * (clip_level / jnp.maximum(norm, clip_level))[None]


def on_chip(*shape):
    return pltpu.VMEM(shape, jnp.float32)


def kept(array):
    return pltpu.with_memory_space_constraint(array, pltpu.VMEM)


def groups(shards):
    runs = shards // RUN
    along_z = [[x * RUN + z * CORES + c for z in range(CHIPS_Z)] for x in range(runs) for c in range(CORES)]
    along_x = [[x * RUN + inner for x in range(runs)] for inner in range(RUN)]
    return along_z, along_x


def on_device(
    grad_out, gate_query, key_input, value_input, decay_rate, pole_angle, residue, skip_gain
):
    rows, width = grad_out.shape
    modes = decay_rate.shape[0]
    shards, chan_shards = lax.axis_size("seq"), lax.axis_size("chan")
    slices = modes * width // HALF
    along_z, along_x = groups(shards)
    where, grad_out = lax.optimization_barrier((lax.axis_index("seq").reshape(1), grad_out))
    scalar = [pl.BlockSpec(memory_space=pltpu.SMEM)]
    whole = pl.BlockSpec(memory_space=pltpu.VMEM)
    packed = pl.pallas_call(
        local_kernel,
        out_shape=on_chip(3 * slices, LANES),
        scratch_shapes=[pltpu.VMEM((rows, width), jnp.float32)] * 2,
        name="local_pass",
    )(grad_out, gate_query, key_input, value_input, decay_rate, pole_angle)
    own = lax.all_to_all(packed, "seq", 0, 0, tiled=True, axis_index_groups=along_z)
    other = lax.ppermute(own, "seq", [(shard, shard ^ 1) for shard in range(shards)])
    message, inside = pl.pallas_call(
        functools.partial(run_kernel, rows),
        in_specs=scalar + [whole] * 4,
        out_shape=(on_chip(3 * SUB * (shards // RUN), LANES), on_chip(CHIPS_Z * SUB, LANES)),
        name="join_run",
    )(where, kept(own), kept(other), decay_rate, pole_angle)
    message = lax.all_to_all(message, "seq", 0, 0, tiled=True, axis_index_groups=along_x)
    answers = pl.pallas_call(
        functools.partial(answer_kernel, rows),
        in_specs=scalar + [whole] * 4,
        out_shape=on_chip(2 * CHIPS_Z * SUB, LANES),
        name="join_runs",
    )(where, kept(message), kept(inside), decay_rate, pole_angle)
    back = kept(lax.all_to_all(answers, "seq", 0, 0, tiled=True, axis_index_groups=along_z))
    raw, squares = pl.pallas_call(
        residue_kernel,
        out_shape=(
            on_chip(2, modes, width),
            on_chip(chan_shards, LANES),
        ),
        name="residue_sums",
    )(back, decay_rate)
    all_squares = kept(lax.all_to_all(squares, "chan", 0, 0, tiled=True))
    grad_key, grad_value = pl.pallas_call(
        signal_kernel,
        out_shape=(jax.ShapeDtypeStruct((rows, width), jnp.bfloat16),) * 2,
        scratch_shapes=[
            pltpu.VMEM((rows, width), jnp.float32),
            pltpu.VMEM((width // LANES, rows * SUB, LANES), jnp.float32),
        ],
        cost_estimate=pl.CostEstimate(flops=20 * rows * width * modes, bytes_accessed=12 * rows * width, transcendentals=0),
        name="signal_pass",
    )(back, grad_out, gate_query, key_input, value_input, decay_rate, pole_angle, residue, skip_gain.reshape(1, width))
    clip_level = math.sqrt(2 * modes * width * chan_shards)
    grad_residue = pl.pallas_call(
        functools.partial(clip_kernel, clip_level),
        out_shape=jax.ShapeDtypeStruct((2, modes, width), jnp.float32),
        name="clip",
    )(all_squares, kept(raw))
    return (grad_key, grad_value, grad_residue)


def solution(mesh):
    return jax.shard_map(
        on_device,
        mesh=mesh,
        in_specs=(
            P("seq", "chan"),
            P("seq", "chan"),
            P("seq", "chan"),
            P("seq", "chan"),
            P(None, "chan"),
            P(None, "chan"),
            P(None, None, "chan"),
            P("chan"),
        ),
        out_specs=(P("seq", "chan"), P("seq", "chan"), P(None, None, "chan")),
        check_vma=False,
    )
```

```python
import functools
import math

import jax
import jax.numpy as jnp
from jax import lax
from jax.experimental import pallas as pl
from jax.experimental.pallas import tpu as pltpu
from jax.sharding import PartitionSpec as P

LANES = 128
HALF = 64
SUB = 8
CORES = 2
CHIPS_Z = 16
RUN = CORES * CHIPS_Z
TURN_PARTS = (1.5703125, 4.837512969970703e-4, 7.54978995489188e-8)


def sine_cosine(angle):
    quarter = jnp.floor(angle * (2.0 / math.pi) + 0.5)
    rest = angle
    for part in TURN_PARTS:
        rest = rest - quarter * part
    square = rest * rest
    sine = ((-1.9515295891e-4 * square + 8.3321608736e-3) * square - 1.6666654611e-1) * square * rest + rest
    cosine = ((2.443315711809948e-5 * square - 1.388731625493765e-3) * square + 4.166664568298827e-2) * square * square
    cosine = cosine - 0.5 * square + 1.0
    index = quarter - 4.0 * jnp.floor(quarter * 0.25)
    odd = (index == 1.0) | (index == 3.0)
    sine_out = jnp.where(odd, cosine, sine)
    cosine_out = jnp.where(odd, sine, cosine)
    sine_out = jnp.where(index >= 2.0, -sine_out, sine_out)
    cosine_out = jnp.where((index == 1.0) | (index == 2.0), -cosine_out, cosine_out)
    return sine_out, cosine_out


def scale_of(decay):
    twice = 2.0 * decay
    series = 1.0 - twice * (1.0 / 7.0)
    for divisor in (6.0, 5.0, 4.0, 3.0, 2.0):
        series = 1.0 - twice * (1.0 / divisor) * series
    return jnp.sqrt(jnp.where(twice < 0.25, twice * series, 1.0 - jnp.exp(-twice)))


def line_block(ref, first, columns=slice(None)):
    block = ref[pl.ds(pl.multiple_of(first, SUB), SUB), columns]
    return [jnp.broadcast_to(block[r : r + 1], block.shape) for r in range(SUB)]


def lane_low(shape):
    return lax.broadcasted_iota(jnp.int32, shape, 1) < HALF


def pack_slices(real, imaginary, store):
    low = lane_low((real.shape[0], LANES))
    for tile in range(real.shape[1] // LANES):
        re = real[:, tile * LANES : (tile + 1) * LANES]
        im = imaginary[:, tile * LANES : (tile + 1) * LANES]
        store(2 * tile, jnp.where(low, re, pltpu.roll(im, HALF, 1)))
        store(2 * tile + 1, jnp.where(low, pltpu.roll(re, HALF, 1), im))


def unpack_slices(load, modes, width):
    low = lane_low((modes, LANES))
    reals, imaginaries = [], []
    for tile in range(width // LANES):
        even, odd = load(2 * tile), load(2 * tile + 1)
        reals.append(jnp.where(low, even, pltpu.roll(odd, HALF, 1)))
        imaginaries.append(jnp.where(low, pltpu.roll(even, HALF, 1), odd))
    return jnp.concatenate(reals, axis=1), jnp.concatenate(imaginaries, axis=1)


def answer_lines(back_ref, part, modes):
    halves = modes // SUB

    def load(block):
        lines = [(block * halves + half) * 2 * SUB + part * SUB for half in range(halves)]
        return jnp.concatenate([back_ref[first : first + SUB] for first in lines], axis=0)

    return load


def product(first, second):
    return first[0] * second[0] - first[1] * second[1], first[0] * second[1] + first[1] * second[0]


def added_product(total, first, second):
    return (
        (total[0] + first[0] * second[0]) - first[1] * second[1],
        (total[1] + first[0] * second[1]) + first[1] * second[0],
    )


def local_kernel(
    grad_ref, gate_ref, key_ref, value_ref, decay_ref, angle_ref,
    packed_ref, weighted, chunk_ref, power_ref, scale_ref, stored,
):
    rows = grad_ref.shape[0]
    modes, width = decay_ref.shape
    weighted[...] = grad_ref[...].astype(jnp.float32) * gate_ref[...].astype(jnp.float32)
    stored[...] = key_ref[...].astype(jnp.float32) * value_ref[...].astype(jnp.float32)
    decay = decay_ref[...]
    sine, cosine = sine_cosine(angle_ref[...])
    radius = jnp.exp(-decay)
    base = (radius * cosine, -radius * sine)
    powers = [base]
    for k in range(2, SUB + 1):
        powers.append(product(powers[k // 2 - 1], powers[k - k // 2 - 1]))
    for k in range(SUB):
        power_ref[2 * k] = powers[k][0]
        power_ref[2 * k + 1] = powers[k][1]
    scale = scale_of(decay)
    scale_ref[...] = scale
    lags = []
    for tile in range(width // LANES):
        cut = slice(tile * LANES, (tile + 1) * LANES)

        def lag_block(j, totals, cut=cut):
            place = pl.ds(pl.multiple_of(j * SUB, SUB), SUB)
            w, s = weighted[place, cut], stored[place, cut]
            return tuple(
                total + s * (w if lag == 0 else pltpu.roll(w, SUB - lag, 0)) for lag, total in enumerate(totals)
            )

        zero = jnp.zeros((SUB, LANES), jnp.float32)
        lags.append(lax.fori_loop(0, rows // SUB, lag_block, (zero,) * SUB, unroll=4))
    place = lax.broadcasted_iota(jnp.int32, (SUB, width), 0)
    lag_sums = []
    for lag in range(SUB):
        line = jnp.concatenate([totals[lag] for totals in lags], axis=1)
        line = jnp.sum(jnp.where(place < SUB - lag, line, 0.0), axis=0, keepdims=True)
        lag_sums.append(jnp.broadcast_to(line, (SUB, width)))
    for first in range(0, modes, SUB):
        part_rows = slice(first, first + SUB)

        def power(k, part_rows=part_rows):
            return power_ref[2 * k - 2, part_rows], power_ref[2 * k - 1, part_rows]

        def block(i, carry, power=power, part_rows=part_rows):
            state, total, reach, far = carry
            j = rows // SUB - 1 - i
            ws, ss = line_block(weighted, j * SUB), line_block(stored, j * SUB)
            eighth = power(SUB)
            chunk_real, chunk_imaginary = ws[0], None
            answer_real, answer_imaginary = ss[0] * eighth[0], ss[0] * eighth[1]
            for k in range(1, SUB):
                real, imaginary = power(k)
                chunk_real = chunk_real + ws[k] * real
                cross = ws[k] * imaginary
                chunk_imaginary = cross if chunk_imaginary is None else chunk_imaginary + cross
                answer_real = answer_real + ss[SUB - k] * real
                answer_imaginary = answer_imaginary + ss[SUB - k] * imaginary
            chunk, answer = (chunk_real, chunk_imaginary), (answer_real, answer_imaginary)
            chunk_ref[2 * j, part_rows] = chunk_real
            chunk_ref[2 * j + 1, part_rows] = chunk_imaginary
            total = added_product(total, answer, state)
            reach = added_product(reach, answer, far)
            return added_product(chunk, eighth, state), total, reach, product(far, eighth)

        zero = jnp.zeros((SUB, width), jnp.float32)
        pair = (zero, zero)
        state, total, reach, _ = lax.fori_loop(
            0, rows // SUB, block, (pair, pair, pair, (jnp.ones((SUB, width), jnp.float32), zero))
        )
        total = total[0] + lag_sums[0], total[1]
        for lag in range(1, SUB):
            real, imaginary = power(lag)
            total = total[0] + lag_sums[lag] * real, total[1] + lag_sums[lag] * imaginary
        own = scale[part_rows]
        total = total[0] * own, total[1] * own
        reach = reach[0] * own, reach[1] * own
        for part, value in enumerate((state, total, reach)):

            def store(block, value, part=part, half=first // SUB):
                line = (block * (modes // SUB) + half) * 3 * SUB + part * SUB
                packed_ref[line : line + SUB] = value

            pack_slices(value[0], value[1], store)


def swap(value):
    return pltpu.roll(value, HALF, 1)


def factors(value, swapped):
    low = lane_low(value.shape)
    return jnp.where(low, value, swapped), jnp.where(low, -swapped, value)


def step(added, state, power):
    direct, cross = power
    here, there = state
    return added[0] + (here * direct + there * cross), added[1] + (there * direct - here * cross)


def squared(power):
    direct, cross = power
    return direct * direct - cross * cross, 2.0 * direct * cross


def place_of(where_ref):
    where = where_ref[0]
    return lax.div(where, RUN), lax.rem(lax.div(where, CORES), CHIPS_Z), lax.rem(where, CORES)


def slice_values(ref, chip):
    modes, width = ref.shape
    halves = modes // SUB
    block, half = lax.div(chip, halves), lax.rem(chip, halves)
    chosen = jnp.zeros((SUB, LANES), jnp.float32)
    for tile in range(width // LANES):
        for first in range(halves):
            here = (lax.div(block, 2) == tile) & (half == first)
            part = ref[first * SUB : (first + 1) * SUB, tile * LANES : (tile + 1) * LANES]
            chosen = jnp.where(here, part, chosen)
    chosen = jnp.where(lane_low(chosen.shape) == (lax.rem(block, 2) == 0), chosen, 0.0)
    return chosen + swap(chosen)


def span_power(span, decay_ref, angle_ref, chip):
    decay, angle = slice_values(decay_ref, chip), slice_values(angle_ref, chip)
    sine, cosine = sine_cosine(angle * float(span))
    radius = jnp.exp(-decay * float(span))
    return radius * cosine, jnp.where(lane_low(sine.shape), radius * sine, -radius * sine)


def run_kernel(span, where_ref, own_ref, other_ref, decay_ref, angle_ref, message_ref, inside_ref):
    _, chip, core = place_of(where_ref)
    power = span_power(span, decay_ref, angle_ref, chip)
    first_core = core == 0

    def tiles(part, z):
        line = (3 * z + part) * SUB
        own, other = own_ref[line : line + SUB], other_ref[line : line + SUB]
        pair = jnp.where(first_core, own, other), jnp.where(first_core, other, own)
        return [(value, swap(value)) for value in pair]

    zero = jnp.zeros((SUB, LANES), jnp.float32)
    state, total, reach = (zero, zero), zero, (zero, zero)
    for z in range(CHIPS_Z):
        for value in tiles(2, z):
            reach = step(value, reach, power)
    for z in reversed(range(CHIPS_Z)):
        carries, sums, reaches = tiles(0, z), tiles(1, z), tiles(2, z)
        inside = []
        for c in reversed(range(CORES)):
            inside.append(state[0])
            direct, cross = factors(*reaches[c])
            total = total + (sums[c][0] + (state[0] * direct + state[1] * cross))
            state = step(carries[c], state, power)
        inside_ref[z * SUB : (z + 1) * SUB] = jnp.where(first_core, inside[1], inside[0])
    copies = message_ref.shape[0] // (3 * SUB)
    for copy in range(copies):
        for part, value in enumerate((state[0], total, reach[0])):
            line = (3 * copy + part) * SUB
            message_ref[line : line + SUB] = value


def answer_kernel(span, where_ref, message_ref, inside_ref, decay_ref, angle_ref, out_ref):
    mine, chip, core = place_of(where_ref)
    power = span_power(span, decay_ref, angle_ref, chip)
    run_power = power
    for _ in range(RUN.bit_length() - 1):
        run_power = squared(run_power)
    zero = jnp.zeros((SUB, LANES), jnp.float32)
    state, total = (zero, zero), zero
    entering = (zero, zero)
    for x in reversed(range(message_ref.shape[0] // (3 * SUB))):
        carry, sums, reach = [message_ref[(3 * x + part) * SUB : (3 * x + part + 1) * SUB] for part in range(3)]
        entering = tuple(jnp.where(mine == x, new, old) for new, old in zip(state, entering))
        direct, cross = factors(reach, swap(reach))
        total = total + (sums + (state[0] * direct + state[1] * cross))
        state = step((carry, swap(carry)), state, run_power)
    moved = step((zero, zero), entering, power)
    entering = tuple(jnp.where(core == CORES - 1, here, there) for here, there in zip(entering, moved))
    chip_power = squared(power)
    for z in reversed(range(CHIPS_Z)):
        out_ref[2 * z * SUB : (2 * z + 1) * SUB] = inside_ref[z * SUB : (z + 1) * SUB] + entering[0]
        out_ref[(2 * z + 1) * SUB : (2 * z + 2) * SUB] = total
        entering = step((zero, zero), entering, chip_power)


def residue_kernel(back_ref, raw_ref, squares_ref):
    _, modes, width = raw_ref.shape
    real, imaginary = unpack_slices(answer_lines(back_ref, 1, modes), modes, width)
    raw_ref[0] = real
    raw_ref[1] = -imaginary
    squares = jnp.sum(real * real + imaginary * imaginary, axis=0, keepdims=True)
    total = squares[:, 0:LANES]
    for tile in range(1, width // LANES):
        total = total + squares[:, tile * LANES : (tile + 1) * LANES]
    squares_ref[...] = jnp.broadcast_to(total, squares_ref.shape)


def signal_kernel(
    back_ref, weighted, chunk_ref, power_ref, scale_ref, key_ref, value_ref, residue_ref, skip_ref,
    grad_key_ref, grad_value_ref, signal,
):
    rows, width = weighted.shape
    modes = scale_ref.shape[0]
    scale = scale_ref[...]
    weight = residue_ref[0] * scale, residue_ref[1] * scale
    place = lax.broadcasted_iota(jnp.int32, (SUB, width), 0)
    taps = []
    for lag in range(SUB):
        if lag:
            tap = weight[0] * power_ref[2 * lag - 2] - weight[1] * power_ref[2 * lag - 1]
        else:
            tap = weight[0]
        line = jnp.broadcast_to(jnp.sum(tap, axis=0, keepdims=True), (SUB, width))
        taps.append(jnp.where(place < SUB - lag, line, 0.0))
    taps[0] = taps[0] + skip_ref[...]
    begin = product(weight, unpack_slices(answer_lines(back_ref, 0, modes), modes, width))
    span = 2 * LANES
    for column in range(0, width, span):
        cut = slice(column, column + span)
        halves = [slice(first, first + SUB) for first in range(0, modes, SUB)]
        scaled = [tuple(part[half, cut] for part in weight) for half in halves]
        start = tuple(tuple(part[half, cut] for part in begin) for half in halves)

        def block(i, states, cut=cut, halves=halves, scaled=scaled):
            j = rows // SUB - 1 - i
            for r in range(SUB):
                k = SUB - r
                total = None
                for half, state in zip(halves, states):
                    part = power_ref[2 * k - 2, half, cut] * state[0] - power_ref[2 * k - 1, half, cut] * state[1]
                    total = part if total is None else total + part
                line = pl.ds(pl.multiple_of((j * SUB + r) * SUB, SUB), SUB)
                for part in range(span // LANES):
                    view = signal.at[cut.start // LANES + part]
                    view[line, :] = total[:, part * LANES : (part + 1) * LANES]
            after = []
            for half, state, factor in zip(halves, states, scaled):
                eighth = power_ref[2 * SUB - 2, half, cut], power_ref[2 * SUB - 1, half, cut]
                chunk = chunk_ref[2 * j, half, cut], chunk_ref[2 * j + 1, half, cut]
                after.append(added_product(product(factor, chunk), eighth, state))
            return tuple(after)

        lax.fori_loop(0, rows // SUB, block, start)
    pair = 2 * SUB
    for tile in range(width // LANES):
        cut = slice(tile * LANES, (tile + 1) * LANES)
        view = signal.at[tile]
        for first in range(0, rows, pair):
            parts = []
            for line in (first, first + SUB):
                w = weighted[line : line + SUB, cut]
                part = taps[0][:, cut] * w
                for lag in range(1, SUB):
                    part = part + taps[lag][:, cut] * pltpu.roll(w, SUB - lag, 0)
                for member in range(SUB):
                    part = part + view[pl.ds(line * SUB + member, SUB, stride=SUB), :]
                parts.append(part)
            part = jnp.concatenate(parts, axis=0)
            both = slice(first, first + pair)
            grad_key_ref[both, cut] = (part * value_ref[both, cut].astype(jnp.float32)).astype(jnp.bfloat16)
            grad_value_ref[both, cut] = (part * key_ref[both, cut].astype(jnp.float32)).astype(jnp.bfloat16)


def clip_kernel(clip_level, squares_ref, raw_ref, out_ref):
    norm = jnp.sqrt(jnp.sum(squares_ref[...], keepdims=True))
    out_ref[...] = raw_ref[...] * (clip_level / jnp.maximum(norm, clip_level))[None]


def on_chip(*shape):
    return pltpu.VMEM(shape, jnp.float32)


def kept(array):
    return pltpu.with_memory_space_constraint(array, pltpu.VMEM)


def groups(shards):
    runs = shards // RUN
    along_z = [[x * RUN + z * CORES + c for z in range(CHIPS_Z)] for x in range(runs) for c in range(CORES)]
    along_x = [[x * RUN + inner for x in range(runs)] for inner in range(RUN)]
    return along_z, along_x


def on_device(
    grad_out, gate_query, key_input, value_input, decay_rate, pole_angle, residue, skip_gain
):
    rows, width = grad_out.shape
    modes = decay_rate.shape[0]
    shards, chan_shards = lax.axis_size("seq"), lax.axis_size("chan")
    slices = modes * width // HALF
    along_z, along_x = groups(shards)
    where, grad_out = lax.optimization_barrier((lax.axis_index("seq").reshape(1), grad_out))
    scalar = [pl.BlockSpec(memory_space=pltpu.SMEM)]
    whole = pl.BlockSpec(memory_space=pltpu.VMEM)
    packed, weighted, chunks, powers, scale = pl.pallas_call(
        local_kernel,
        out_shape=(
            on_chip(3 * slices, LANES),
            on_chip(rows, width),
            on_chip(2 * rows // SUB, modes, width),
            on_chip(2 * SUB, modes, width),
            on_chip(modes, width),
        ),
        scratch_shapes=[pltpu.VMEM((rows, width), jnp.float32)],
        name="local_pass",
    )(grad_out, gate_query, key_input, value_input, decay_rate, pole_angle)
    own = lax.all_to_all(packed, "seq", 0, 0, tiled=True, axis_index_groups=along_z)
    other = lax.ppermute(own, "seq", [(shard, shard ^ 1) for shard in range(shards)])
    message, inside = pl.pallas_call(
        functools.partial(run_kernel, rows),
        in_specs=scalar + [whole] * 4,
        out_shape=(on_chip(3 * SUB * (shards // RUN), LANES), on_chip(CHIPS_Z * SUB, LANES)),
        name="join_run",
    )(where, kept(own), kept(other), decay_rate, pole_angle)
    message = lax.all_to_all(message, "seq", 0, 0, tiled=True, axis_index_groups=along_x)
    answers = pl.pallas_call(
        functools.partial(answer_kernel, rows),
        in_specs=scalar + [whole] * 4,
        out_shape=on_chip(2 * CHIPS_Z * SUB, LANES),
        name="join_runs",
    )(where, kept(message), kept(inside), decay_rate, pole_angle)
    back = kept(lax.all_to_all(answers, "seq", 0, 0, tiled=True, axis_index_groups=along_z))
    raw, squares = pl.pallas_call(
        residue_kernel,
        out_shape=(
            on_chip(2, modes, width),
            on_chip(chan_shards, LANES),
        ),
        name="residue_sums",
    )(back)
    all_squares = kept(lax.all_to_all(squares, "chan", 0, 0, tiled=True))
    grad_key, grad_value = pl.pallas_call(
        signal_kernel,
        out_shape=(jax.ShapeDtypeStruct((rows, width), jnp.bfloat16),) * 2,
        scratch_shapes=[pltpu.VMEM((width // LANES, rows * SUB, LANES), jnp.float32)],
        cost_estimate=pl.CostEstimate(flops=20 * rows * width * modes, bytes_accessed=12 * rows * width, transcendentals=0),
        name="signal_pass",
    )(
        back, kept(weighted), kept(chunks), kept(powers), kept(scale), kept(key_input), kept(value_input),
        kept(residue), skip_gain.reshape(1, width),
    )
    clip_level = math.sqrt(2 * modes * width * chan_shards)
    grad_residue = pl.pallas_call(
        functools.partial(clip_kernel, clip_level),
        out_shape=jax.ShapeDtypeStruct((2, modes, width), jnp.float32),
        name="clip",
    )(all_squares, kept(raw))
    return (grad_key, grad_value, grad_residue)


def solution(mesh):
    return jax.shard_map(
        on_device,
        mesh=mesh,
        in_specs=(
            P("seq", "chan"),
            P("seq", "chan"),
            P("seq", "chan"),
            P("seq", "chan"),
            P(None, "chan"),
            P(None, "chan"),
            P(None, None, "chan"),
            P("chan"),
        ),
        out_specs=(P("seq", "chan"), P("seq", "chan"), P(None, None, "chan")),
        check_vma=False,
    )
```

```python
import functools
import math

import jax
import jax.numpy as jnp
from jax import lax
from jax.experimental import pallas as pl
from jax.experimental.pallas import tpu as pltpu
from jax.sharding import Mesh, PartitionSpec as P

LANES = 128
HALF = 64
SUB = 8
CORES = 2
CHIPS_Z = 16
RUN = CORES * CHIPS_Z
PART = 4
SEQ = ("chip", "core")
TURN_PARTS = (1.5703125, 4.837512969970703e-4, 7.54978995489188e-8)


def sine_cosine(angle):
    quarter = jnp.floor(angle * (2.0 / math.pi) + 0.5)
    rest = angle
    for part in TURN_PARTS:
        rest = rest - quarter * part
    square = rest * rest
    sine = ((-1.9515295891e-4 * square + 8.3321608736e-3) * square - 1.6666654611e-1) * square * rest + rest
    cosine = ((2.443315711809948e-5 * square - 1.388731625493765e-3) * square + 4.166664568298827e-2) * square * square
    cosine = cosine - 0.5 * square + 1.0
    index = quarter - 4.0 * jnp.floor(quarter * 0.25)
    odd = (index == 1.0) | (index == 3.0)
    sine_out = jnp.where(odd, cosine, sine)
    cosine_out = jnp.where(odd, sine, cosine)
    sine_out = jnp.where(index >= 2.0, -sine_out, sine_out)
    cosine_out = jnp.where((index == 1.0) | (index == 2.0), -cosine_out, cosine_out)
    return sine_out, cosine_out


def scale_of(decay):
    twice = 2.0 * decay
    series = 1.0 - twice * (1.0 / 7.0)
    for divisor in (6.0, 5.0, 4.0, 3.0, 2.0):
        series = 1.0 - twice * (1.0 / divisor) * series
    return jnp.sqrt(jnp.where(twice < 0.25, twice * series, 1.0 - jnp.exp(-twice)))


def line_block(ref, first, columns=slice(None)):
    block = ref[pl.ds(pl.multiple_of(first, SUB), SUB), columns]
    return [jnp.broadcast_to(block[r : r + 1], block.shape) for r in range(SUB)]


def lane_low(shape):
    return lax.broadcasted_iota(jnp.int32, shape, 1) < HALF


def pack_slices(real, imaginary, store):
    low = lane_low((real.shape[0], LANES))
    for tile in range(real.shape[1] // LANES):
        re = real[:, tile * LANES : (tile + 1) * LANES]
        im = imaginary[:, tile * LANES : (tile + 1) * LANES]
        store(2 * tile, jnp.where(low, re, pltpu.roll(im, HALF, 1)))
        store(2 * tile + 1, jnp.where(low, pltpu.roll(re, HALF, 1), im))


def unpack_slices(load, modes, width):
    low = lane_low((modes, LANES))
    reals, imaginaries = [], []
    for tile in range(width // LANES):
        even, odd = load(2 * tile), load(2 * tile + 1)
        reals.append(jnp.where(low, even, pltpu.roll(odd, HALF, 1)))
        imaginaries.append(jnp.where(low, pltpu.roll(even, HALF, 1), odd))
    return jnp.concatenate(reals, axis=1), jnp.concatenate(imaginaries, axis=1)


def slice_lines(ref, part, parts):
    def load(block):
        lines = [((2 * block + half) * parts + part) * PART for half in range(2)]
        return jnp.concatenate([ref[first : first + PART] for first in lines], axis=0)

    return load


def product(first, second):
    return first[0] * second[0] - first[1] * second[1], first[0] * second[1] + first[1] * second[0]


def added_product(total, first, second):
    return (
        (total[0] + first[0] * second[0]) - first[1] * second[1],
        (total[1] + first[0] * second[1]) + first[1] * second[0],
    )


def local_kernel(
    where_ref, grad_ref, gate_ref, key_ref, value_ref, decay_ref, angle_ref,
    keep_ref, send_ref, weighted, chunk_ref, power_ref, scale_ref, stored,
):
    rows = grad_ref.shape[0]
    modes, width = decay_ref.shape
    weighted[...] = grad_ref[...].astype(jnp.float32) * gate_ref[...].astype(jnp.float32)
    stored[...] = key_ref[...].astype(jnp.float32) * value_ref[...].astype(jnp.float32)
    decay = decay_ref[...]
    sine, cosine = sine_cosine(angle_ref[...])
    radius = jnp.exp(-decay)
    base = (radius * cosine, -radius * sine)
    powers = [base]
    for k in range(2, SUB + 1):
        powers.append(product(powers[k // 2 - 1], powers[k - k // 2 - 1]))
    for k in range(SUB):
        power_ref[2 * k] = powers[k][0]
        power_ref[2 * k + 1] = powers[k][1]
    scale = scale_of(decay)
    scale_ref[...] = scale
    lags = []
    for tile in range(width // LANES):
        cut = slice(tile * LANES, (tile + 1) * LANES)

        def lag_block(j, totals, cut=cut):
            place = pl.ds(pl.multiple_of(j * SUB, SUB), SUB)
            w, s = weighted[place, cut], stored[place, cut]
            return tuple(
                total + s * (w if lag == 0 else pltpu.roll(w, SUB - lag, 0)) for lag, total in enumerate(totals)
            )

        zero = jnp.zeros((SUB, LANES), jnp.float32)
        lags.append(lax.fori_loop(0, rows // SUB, lag_block, (zero,) * SUB, unroll=4))
    place = lax.broadcasted_iota(jnp.int32, (SUB, width), 0)
    lag_sums = []
    for lag in range(SUB):
        line = jnp.concatenate([totals[lag] for totals in lags], axis=1)
        line = jnp.sum(jnp.where(place < SUB - lag, line, 0.0), axis=0, keepdims=True)
        lag_sums.append(jnp.broadcast_to(line, (SUB, width)))
    results = []
    for first in range(0, modes, SUB):
        part_rows = slice(first, first + SUB)

        def power(k, part_rows=part_rows):
            return power_ref[2 * k - 2, part_rows], power_ref[2 * k - 1, part_rows]

        def block(i, carry, power=power, part_rows=part_rows):
            state, total, reach, far = carry
            j = rows // SUB - 1 - i
            ws, ss = line_block(weighted, j * SUB), line_block(stored, j * SUB)
            eighth = power(SUB)
            chunk_real, chunk_imaginary = ws[0], None
            answer_real, answer_imaginary = ss[0] * eighth[0], ss[0] * eighth[1]
            for k in range(1, SUB):
                real, imaginary = power(k)
                chunk_real = chunk_real + ws[k] * real
                cross = ws[k] * imaginary
                chunk_imaginary = cross if chunk_imaginary is None else chunk_imaginary + cross
                answer_real = answer_real + ss[SUB - k] * real
                answer_imaginary = answer_imaginary + ss[SUB - k] * imaginary
            chunk, answer = (chunk_real, chunk_imaginary), (answer_real, answer_imaginary)
            chunk_ref[2 * j, part_rows] = chunk_real
            chunk_ref[2 * j + 1, part_rows] = chunk_imaginary
            total = added_product(total, answer, state)
            reach = added_product(reach, answer, far)
            return added_product(chunk, eighth, state), total, reach, product(far, eighth)

        zero = jnp.zeros((SUB, width), jnp.float32)
        pair = (zero, zero)
        state, total, reach, _ = lax.fori_loop(
            0, rows // SUB, block, (pair, pair, pair, (jnp.ones((SUB, width), jnp.float32), zero))
        )
        total = total[0] + lag_sums[0], total[1]
        for lag in range(1, SUB):
            real, imaginary = power(lag)
            total = total[0] + lag_sums[lag] * real, total[1] + lag_sums[lag] * imaginary
        own = scale[part_rows]
        total = total[0] * own, total[1] * own
        reach = reach[0] * own, reach[1] * own
        results.append(state + total + reach)
    first_core = core_of(where_ref) == 0
    for part, (lower, upper) in enumerate(zip(*results)):
        keep_ref[part] = jnp.where(first_core, lower, upper)
        send_ref[part] = jnp.where(first_core, upper, lower)


def shard_power(power_ref, first_core, rows):
    real, imaginary = power_ref[2 * SUB - 2], power_ref[2 * SUB - 1]
    power = tuple(jnp.where(first_core, part[:SUB], part[SUB:]) for part in (real, imaginary))
    for _ in range((rows // SUB).bit_length() - 1):
        power = product(power, power)
    return power


def chip_kernel(rows, where_ref, keep_ref, got_ref, power_ref, packed_ref):
    first_core = core_of(where_ref) == 0
    power = shard_power(power_ref, first_core, rows)
    early = [jnp.where(first_core, keep_ref[part], got_ref[part]) for part in range(6)]
    late = [jnp.where(first_core, got_ref[part], keep_ref[part]) for part in range(6)]
    carry = added_product((early[0], early[1]), power, (late[0], late[1]))
    total = added_product((early[2] + late[2], early[3] + late[3]), (early[4], early[5]), (late[0], late[1]))
    reach = added_product((late[4], late[5]), power, (early[4], early[5]))
    for part, value in enumerate((carry, total, reach)):

        def store(block, value, part=part):
            for half in range(2):
                line = ((2 * block + half) * 3 + part) * PART
                packed_ref[line : line + PART] = value[half * PART : (half + 1) * PART]

        pack_slices(value[0], value[1], store)


def swap(value):
    return pltpu.roll(value, HALF, 1)


def factors(value, swapped):
    low = lane_low(value.shape)
    return jnp.where(low, value, swapped), jnp.where(low, -swapped, value)


def step(added, state, power):
    direct, cross = power
    here, there = state
    return added[0] + (here * direct + there * cross), added[1] + (there * direct - here * cross)


def squared(power):
    direct, cross = power
    return direct * direct - cross * cross, 2.0 * direct * cross


def core_of(where_ref):
    return lax.rem(where_ref[0], CORES)


def slice_values(ref, where_ref):
    modes, width = ref.shape
    chip, core = lax.rem(lax.div(where_ref[0], CORES), CHIPS_Z), core_of(where_ref)
    block, half = lax.div(chip, 2), lax.rem(chip, 2)
    chosen = jnp.zeros((PART, LANES), jnp.float32)
    for tile in range(width // LANES):
        for first in range(0, modes, PART):
            here = (lax.div(block, 2) == tile) & (core * SUB + half * PART == first)
            chosen = jnp.where(here, ref[first : first + PART, tile * LANES : (tile + 1) * LANES], chosen)
    chosen = jnp.where(lane_low(chosen.shape) == (lax.rem(block, 2) == 0), chosen, 0.0)
    return chosen + swap(chosen)


def span_power(span, decay_ref, angle_ref, where_ref):
    decay, angle = slice_values(decay_ref, where_ref), slice_values(angle_ref, where_ref)
    sine, cosine = sine_cosine(angle * float(span))
    radius = jnp.exp(-decay * float(span))
    return radius * cosine, jnp.where(lane_low(sine.shape), radius * sine, -radius * sine)


def lines_of(ref, place):
    return ref[place * PART : (place + 1) * PART]


def run_kernel(span, where_ref, own_ref, decay_ref, angle_ref, message_ref, inside_ref, power_ref):
    power = span_power(span, decay_ref, angle_ref, where_ref)
    power_ref[0:PART], power_ref[PART:] = power
    zero = jnp.zeros((PART, LANES), jnp.float32)
    state, total, reach = (zero, zero), zero, (zero, zero)
    reaches = []
    for z in range(CHIPS_Z):
        value = lines_of(own_ref, 3 * z + 2)
        reaches.append((value, swap(value)))
        reach = step(reaches[z], reach, power)
    for z in reversed(range(CHIPS_Z)):
        carry = lines_of(own_ref, 3 * z)
        inside_ref[z * PART : (z + 1) * PART] = state[0]
        direct, cross = factors(*reaches[z])
        total = total + (lines_of(own_ref, 3 * z + 1) + (state[0] * direct + state[1] * cross))
        state = step((carry, swap(carry)), state, power)
    for copy in range(message_ref.shape[0] // (3 * PART)):
        for part, value in enumerate((state[0], total, reach[0])):
            line = (3 * copy + part) * PART
            message_ref[line : line + PART] = value


def answer_kernel(where_ref, message_ref, inside_ref, power_ref, out_ref):
    mine = lax.div(where_ref[0], RUN)
    power = power_ref[0:PART], power_ref[PART:]
    run_power = power
    for _ in range(CHIPS_Z.bit_length() - 1):
        run_power = squared(run_power)
    zero = jnp.zeros((PART, LANES), jnp.float32)
    state, total = (zero, zero), zero
    entering = (zero, zero)
    for x in reversed(range(message_ref.shape[0] // (3 * PART))):
        carry, sums, reach = [lines_of(message_ref, 3 * x + part) for part in range(3)]
        entering = tuple(jnp.where(mine == x, new, old) for new, old in zip(state, entering))
        direct, cross = factors(reach, swap(reach))
        total = total + (sums + (state[0] * direct + state[1] * cross))
        state = step((carry, swap(carry)), state, run_power)
    for z in reversed(range(CHIPS_Z)):
        out_ref[2 * z * PART : (2 * z + 1) * PART] = lines_of(inside_ref, z) + entering[0]
        out_ref[(2 * z + 1) * PART : (2 * z + 2) * PART] = total
        entering = step((zero, zero), entering, power)


def residue_kernel(rows, where_ref, back_ref, keep_ref, got_ref, power_ref, mine_ref, send_ref, squares_ref):
    _, modes, width = mine_ref.shape
    first_core = core_of(where_ref) == 0
    power = shard_power(power_ref, first_core, rows)
    late = unpack_slices(slice_lines(back_ref, 0, 2), modes, width)
    carry = tuple(jnp.where(first_core, got_ref[part], keep_ref[part]) for part in range(2))
    early = added_product(carry, power, late)
    real, imaginary = unpack_slices(slice_lines(back_ref, 1, 2), modes, width)
    for part in range(2):
        mine_ref[part] = jnp.where(first_core, early[part], late[part])
        send_ref[part] = jnp.where(first_core, late[part], early[part])
    for ref in (mine_ref, send_ref):
        ref[2] = real
        ref[3] = -imaginary
    squares = jnp.sum(real * real + imaginary * imaginary, axis=0, keepdims=True)
    total = squares[:, 0:LANES]
    for tile in range(1, width // LANES):
        total = total + squares[:, tile * LANES : (tile + 1) * LANES]
    squares_ref[...] = jnp.broadcast_to(total, squares_ref.shape)


def both_halves(where_ref, mine_ref, other_ref, part):
    first_core = core_of(where_ref) == 0
    mine, other = mine_ref[part], other_ref[part]
    return jnp.concatenate([jnp.where(first_core, mine, other), jnp.where(first_core, other, mine)], axis=0)


def signal_kernel(
    where_ref, mine_ref, other_ref, weighted, chunk_ref, power_ref, scale_ref, key_ref, value_ref, residue_ref, skip_ref,
    grad_key_ref, grad_value_ref, signal,
):
    rows, width = weighted.shape
    modes = scale_ref.shape[0]
    scale = scale_ref[...]
    weight = residue_ref[0] * scale, residue_ref[1] * scale
    place = lax.broadcasted_iota(jnp.int32, (SUB, width), 0)
    taps = []
    for lag in range(SUB):
        if lag:
            tap = weight[0] * power_ref[2 * lag - 2] - weight[1] * power_ref[2 * lag - 1]
        else:
            tap = weight[0]
        line = jnp.broadcast_to(jnp.sum(tap, axis=0, keepdims=True), (SUB, width))
        taps.append(jnp.where(place < SUB - lag, line, 0.0))
    taps[0] = taps[0] + skip_ref[...]
    begin = product(weight, tuple(both_halves(where_ref, mine_ref, other_ref, part) for part in range(2)))
    span = 2 * LANES
    for column in range(0, width, span):
        cut = slice(column, column + span)
        halves = [slice(first, first + SUB) for first in range(0, modes, SUB)]
        scaled = [tuple(part[half, cut] for part in weight) for half in halves]
        start = tuple(tuple(part[half, cut] for part in begin) for half in halves)

        def block(i, states, cut=cut, halves=halves, scaled=scaled):
            j = rows // SUB - 1 - i
            for r in range(SUB):
                k = SUB - r
                total = None
                for half, state in zip(halves, states):
                    part = power_ref[2 * k - 2, half, cut] * state[0] - power_ref[2 * k - 1, half, cut] * state[1]
                    total = part if total is None else total + part
                line = pl.ds(pl.multiple_of((j * SUB + r) * SUB, SUB), SUB)
                for part in range(span // LANES):
                    view = signal.at[cut.start // LANES + part]
                    view[line, :] = total[:, part * LANES : (part + 1) * LANES]
            after = []
            for half, state, factor in zip(halves, states, scaled):
                eighth = power_ref[2 * SUB - 2, half, cut], power_ref[2 * SUB - 1, half, cut]
                chunk = chunk_ref[2 * j, half, cut], chunk_ref[2 * j + 1, half, cut]
                after.append(added_product(product(factor, chunk), eighth, state))
            return tuple(after)

        lax.fori_loop(0, rows // SUB, block, start)
    pair = 2 * SUB
    for tile in range(width // LANES):
        cut = slice(tile * LANES, (tile + 1) * LANES)
        view = signal.at[tile]
        for first in range(0, rows, pair):
            parts = []
            for line in (first, first + SUB):
                w = weighted[line : line + SUB, cut]
                part = taps[0][:, cut] * w
                for lag in range(1, SUB):
                    part = part + taps[lag][:, cut] * pltpu.roll(w, SUB - lag, 0)
                for member in range(SUB):
                    part = part + view[pl.ds(line * SUB + member, SUB, stride=SUB), :]
                parts.append(part)
            part = jnp.concatenate(parts, axis=0)
            both = slice(first, first + pair)
            grad_key_ref[both, cut] = (part * value_ref[both, cut].astype(jnp.float32)).astype(jnp.bfloat16)
            grad_value_ref[both, cut] = (part * key_ref[both, cut].astype(jnp.float32)).astype(jnp.bfloat16)


def clip_kernel(clip_level, where_ref, squares_ref, mine_ref, other_ref, after_ref, out_ref):
    del after_ref
    norm = jnp.sqrt(jnp.sum(squares_ref[...], keepdims=True))
    factor = clip_level / jnp.maximum(norm, clip_level)
    for part in range(2):
        out_ref[part] = both_halves(where_ref, mine_ref, other_ref, 2 + part) * factor


def on_chip(*shape):
    return pltpu.VMEM(shape, jnp.float32)


def kept(array):
    return pltpu.with_memory_space_constraint(array, pltpu.VMEM)


def groups(shards):
    runs = shards // RUN
    along_z = [[x * RUN + z * CORES + c for z in range(CHIPS_Z)] for x in range(runs) for c in range(CORES)]
    along_x = [[x * RUN + inner for x in range(runs)] for inner in range(RUN)]
    return along_z, along_x


def on_device(
    grad_out, gate_query, key_input, value_input, decay_rate, pole_angle, residue, skip_gain
):
    rows, width = grad_out.shape
    modes = decay_rate.shape[0]
    shards, chan_shards = lax.axis_size(SEQ), lax.axis_size("chan")
    runs = shards // RUN
    along_z, along_x = groups(shards)
    flip = [(shard, shard ^ 1) for shard in range(shards)]
    where, grad_out = lax.optimization_barrier((lax.axis_index(SEQ).reshape(1), grad_out))
    scalar = pl.BlockSpec(memory_space=pltpu.SMEM)
    whole = pl.BlockSpec(memory_space=pltpu.VMEM)
    keep, send, weighted, chunks, powers, scale = pl.pallas_call(
        local_kernel,
        in_specs=[scalar] + [whole] * 6,
        out_shape=(
            on_chip(6, SUB, width),
            on_chip(6, SUB, width),
            on_chip(rows, width),
            on_chip(2 * rows // SUB, modes, width),
            on_chip(2 * SUB, modes, width),
            on_chip(modes, width),
        ),
        scratch_shapes=[pltpu.VMEM((rows, width), jnp.float32)],
        name="local_pass",
    )(where, grad_out, gate_query, key_input, value_input, decay_rate, pole_angle)
    keep, powers = kept(keep), kept(powers)
    got = kept(lax.ppermute(send, SEQ, flip))
    packed = pl.pallas_call(
        functools.partial(chip_kernel, rows),
        in_specs=[scalar] + [whole] * 3,
        out_shape=on_chip(3 * CHIPS_Z * PART, LANES),
        name="join_chip",
    )(where, keep, got, powers)
    own = kept(exchange(packed, CHIPS_Z, along_z))
    message, inside, power = pl.pallas_call(
        functools.partial(run_kernel, CORES * rows),
        in_specs=[scalar] + [whole] * 3,
        out_shape=(on_chip(3 * PART * runs, LANES), on_chip(CHIPS_Z * PART, LANES), on_chip(2 * PART, LANES)),
        name="join_run",
    )(where, own, kept(decay_rate), kept(pole_angle))
    message = kept(exchange(message, runs, along_x))
    answers = pl.pallas_call(
        answer_kernel,
        in_specs=[scalar] + [whole] * 3,
        out_shape=on_chip(2 * CHIPS_Z * PART, LANES),
        name="join_runs",
    )(where, message, kept(inside), kept(power))
    back = kept(exchange(answers, CHIPS_Z, along_z))
    mine, send, squares = pl.pallas_call(
        functools.partial(residue_kernel, rows),
        in_specs=[scalar] + [whole] * 4,
        out_shape=(
            on_chip(4, SUB, width),
            on_chip(4, SUB, width),
            on_chip(CORES * chan_shards, LANES),
        ),
        name="residue_sums",
    )(where, back, keep, got, powers)
    other = kept(lax.ppermute(send, SEQ, flip))
    mine = kept(mine)
    all_squares = kept(lax.all_to_all(squares, ("core", "chan"), 0, 0, tiled=True))
    grad_key, grad_value = pl.pallas_call(
        signal_kernel,
        in_specs=[scalar] + [whole] * 10,
        out_shape=(jax.ShapeDtypeStruct((rows, width), jnp.bfloat16),) * 2,
        scratch_shapes=[pltpu.VMEM((width // LANES, rows * SUB, LANES), jnp.float32)],
        cost_estimate=pl.CostEstimate(flops=20 * rows * width * modes, bytes_accessed=12 * rows * width, transcendentals=0),
        name="signal_pass",
    )(
        where, mine, other, kept(weighted), kept(chunks), powers, kept(scale), kept(key_input), kept(value_input),
        kept(residue), skip_gain.reshape(1, width),
    )
    clip_level = math.sqrt(2 * modes * width * chan_shards)
    grad_residue = pl.pallas_call(
        functools.partial(clip_kernel, clip_level),
        in_specs=[scalar] + [whole] * 3 + [pl.BlockSpec(memory_space=pl.ANY)],
        out_shape=jax.ShapeDtypeStruct((2, modes, width), jnp.float32),
        name="clip",
    )(where, all_squares, mine, other, grad_key)
    return (grad_key, grad_value, grad_residue)


def exchange(array, members, over):
    sent = array.reshape(members, -1)
    return lax.all_to_all(sent, SEQ, 0, 0, tiled=True, axis_index_groups=over).reshape(array.shape)


def solution(mesh):
    shards, chan_shards = mesh.devices.shape
    split = Mesh(mesh.devices.reshape(shards // CORES, CORES, chan_shards), ("chip", "core", "chan"))
    return jax.shard_map(
        on_device,
        mesh=split,
        in_specs=(
            P(SEQ, "chan"),
            P(SEQ, "chan"),
            P(SEQ, "chan"),
            P(SEQ, "chan"),
            P(None, "chan"),
            P(None, "chan"),
            P(None, None, "chan"),
            P("chan"),
        ),
        out_specs=(P(SEQ, "chan"), P(SEQ, "chan"), P(None, None, "chan")),
        check_vma=False,
    )
```

```python
import functools
import math

import jax
import jax.numpy as jnp
from jax import lax
from jax.experimental import pallas as pl
from jax.experimental.pallas import tpu as pltpu
from jax.sharding import Mesh, PartitionSpec as P

LANES = 128
HALF = 64
SUB = 8
CORES = 2
CHIPS_Z = 16
RUN = CORES * CHIPS_Z
PART = 4
SEQ = ("chip", "core")
TURN_PARTS = (1.5703125, 4.837512969970703e-4, 7.54978995489188e-8)


def sine_cosine(angle):
    quarter = jnp.floor(angle * (2.0 / math.pi) + 0.5)
    rest = angle
    for part in TURN_PARTS:
        rest = rest - quarter * part
    square = rest * rest
    sine = ((-1.9515295891e-4 * square + 8.3321608736e-3) * square - 1.6666654611e-1) * square * rest + rest
    cosine = ((2.443315711809948e-5 * square - 1.388731625493765e-3) * square + 4.166664568298827e-2) * square * square
    cosine = cosine - 0.5 * square + 1.0
    index = quarter - 4.0 * jnp.floor(quarter * 0.25)
    odd = (index == 1.0) | (index == 3.0)
    sine_out = jnp.where(odd, cosine, sine)
    cosine_out = jnp.where(odd, sine, cosine)
    sine_out = jnp.where(index >= 2.0, -sine_out, sine_out)
    cosine_out = jnp.where((index == 1.0) | (index == 2.0), -cosine_out, cosine_out)
    return sine_out, cosine_out


def scale_of(decay):
    twice = 2.0 * decay
    series = 1.0 - twice * (1.0 / 7.0)
    for divisor in (6.0, 5.0, 4.0, 3.0, 2.0):
        series = 1.0 - twice * (1.0 / divisor) * series
    return jnp.sqrt(jnp.where(twice < 0.25, twice * series, 1.0 - jnp.exp(-twice)))


def line_block(ref, first, columns=slice(None)):
    block = ref[pl.ds(pl.multiple_of(first, SUB), SUB), columns]
    return [jnp.broadcast_to(block[r : r + 1], block.shape) for r in range(SUB)]


def lane_low(shape):
    return lax.broadcasted_iota(jnp.int32, shape, 1) < HALF


def pack_slices(real, imaginary, store):
    low = lane_low((real.shape[0], LANES))
    for tile in range(real.shape[1] // LANES):
        re = real[:, tile * LANES : (tile + 1) * LANES]
        im = imaginary[:, tile * LANES : (tile + 1) * LANES]
        store(2 * tile, jnp.where(low, re, pltpu.roll(im, HALF, 1)))
        store(2 * tile + 1, jnp.where(low, pltpu.roll(re, HALF, 1), im))


def unpack_slices(load, modes, width):
    low = lane_low((modes, LANES))
    reals, imaginaries = [], []
    for tile in range(width // LANES):
        even, odd = load(2 * tile), load(2 * tile + 1)
        reals.append(jnp.where(low, even, pltpu.roll(odd, HALF, 1)))
        imaginaries.append(jnp.where(low, pltpu.roll(even, HALF, 1), odd))
    return jnp.concatenate(reals, axis=1), jnp.concatenate(imaginaries, axis=1)


def slice_lines(ref, part, parts):
    def load(block):
        lines = [((2 * block + half) * parts + part) * PART for half in range(2)]
        return jnp.concatenate([ref[first : first + PART] for first in lines], axis=0)

    return load


def product(first, second):
    return first[0] * second[0] - first[1] * second[1], first[0] * second[1] + first[1] * second[0]


def added_product(total, first, second):
    return (
        (total[0] + first[0] * second[0]) - first[1] * second[1],
        (total[1] + first[0] * second[1]) + first[1] * second[0],
    )


def chosen_half(first, array):
    half = array.shape[0] // 2
    return jnp.where(first, array[:half], array[half:])


def half_pass(weighted, stored, lag_sums, base, scale, result_ref, chunk_ref, power_ref):
    rows, width = weighted.shape
    powers = [base]
    for k in range(2, SUB + 1):
        powers.append(product(powers[k // 2 - 1], powers[k - k // 2 - 1]))
    for k in range(SUB):
        power_ref[2 * k], power_ref[2 * k + 1] = powers[k]

    def power(k):
        return power_ref[2 * k - 2], power_ref[2 * k - 1]

    def block(i, carry):
        state, total, reach, far = carry
        j = rows // SUB - 1 - i
        ws, ss = line_block(weighted, j * SUB), line_block(stored, j * SUB)
        eighth = power(SUB)
        chunk_real, chunk_imaginary = ws[0], None
        answer_real, answer_imaginary = ss[0] * eighth[0], ss[0] * eighth[1]
        for k in range(1, SUB):
            real, imaginary = power(k)
            chunk_real = chunk_real + ws[k] * real
            cross = ws[k] * imaginary
            chunk_imaginary = cross if chunk_imaginary is None else chunk_imaginary + cross
            answer_real = answer_real + ss[SUB - k] * real
            answer_imaginary = answer_imaginary + ss[SUB - k] * imaginary
        chunk, answer = (chunk_real, chunk_imaginary), (answer_real, answer_imaginary)
        chunk_ref[2 * j] = chunk_real
        chunk_ref[2 * j + 1] = chunk_imaginary
        total = added_product(total, answer, state)
        reach = added_product(reach, answer, far)
        return added_product(chunk, eighth, state), total, reach, product(far, eighth)

    zero = jnp.zeros((SUB, width), jnp.float32)
    pair = (zero, zero)
    state, total, reach, _ = lax.fori_loop(
        0, rows // SUB, block, (pair, pair, pair, (jnp.ones((SUB, width), jnp.float32), zero))
    )
    total = total[0] + lag_sums[0], total[1]
    for lag in range(1, SUB):
        real, imaginary = power(lag)
        total = total[0] + lag_sums[lag] * real, total[1] + lag_sums[lag] * imaginary
    result_ref[0], result_ref[1] = state
    for part in range(2):
        result_ref[2 + part] = total[part] * scale
        result_ref[4 + part] = reach[part] * scale


def first_kernel(
    where_ref, grad_ref, gate_ref, key_ref, value_ref, decay_ref, angle_ref,
    send_ref, chunk_ref, power_ref, weighted, stored, lag_ref, base_ref, scale_ref,
):
    rows, width = grad_ref.shape
    weighted[...] = grad_ref[...].astype(jnp.float32) * gate_ref[...].astype(jnp.float32)
    stored[...] = key_ref[...].astype(jnp.float32) * value_ref[...].astype(jnp.float32)
    decay = decay_ref[...]
    sine, cosine = sine_cosine(angle_ref[...])
    radius = jnp.exp(-decay)
    base = (radius * cosine, -radius * sine)
    scale = scale_of(decay)
    first_core = core_of(where_ref) == 0
    base_ref[0], base_ref[1] = [chosen_half(first_core, part) for part in base]
    scale_ref[...] = chosen_half(first_core, scale)
    lags = []
    for tile in range(width // LANES):
        cut = slice(tile * LANES, (tile + 1) * LANES)

        def lag_block(j, totals, cut=cut):
            place = pl.ds(pl.multiple_of(j * SUB, SUB), SUB)
            w, s = weighted[place, cut], stored[place, cut]
            return tuple(
                total + s * (w if lag == 0 else pltpu.roll(w, SUB - lag, 0)) for lag, total in enumerate(totals)
            )

        zero = jnp.zeros((SUB, LANES), jnp.float32)
        lags.append(lax.fori_loop(0, rows // SUB, lag_block, (zero,) * SUB, unroll=4))
    place = lax.broadcasted_iota(jnp.int32, (SUB, width), 0)
    lag_sums = []
    for lag in range(SUB):
        line = jnp.concatenate([totals[lag] for totals in lags], axis=1)
        line = jnp.sum(jnp.where(place < SUB - lag, line, 0.0), axis=0, keepdims=True)
        lag_sums.append(jnp.broadcast_to(line, (SUB, width)))
        lag_ref[lag] = lag_sums[lag]
    other = core_of(where_ref) != 0
    half_pass(
        weighted, stored, lag_sums, tuple(chosen_half(other, part) for part in base), chosen_half(other, scale),
        send_ref, chunk_ref, power_ref,
    )


def second_kernel(weighted, stored, lag_ref, base_ref, scale_ref, keep_ref, chunk_ref, power_ref):
    lag_sums = [lag_ref[lag] for lag in range(SUB)]
    half_pass(
        weighted, stored, lag_sums, (base_ref[0], base_ref[1]), scale_ref[...], keep_ref, chunk_ref, power_ref
    )


def shard_power(power_ref, rows):
    power = power_ref[2 * SUB - 2], power_ref[2 * SUB - 1]
    for _ in range((rows // SUB).bit_length() - 1):
        power = product(power, power)
    return power


def chip_kernel(rows, where_ref, keep_ref, got_ref, power_ref, packed_ref):
    first_core = core_of(where_ref) == 0
    power = shard_power(power_ref, rows)
    early = [jnp.where(first_core, keep_ref[part], got_ref[part]) for part in range(6)]
    late = [jnp.where(first_core, got_ref[part], keep_ref[part]) for part in range(6)]
    carry = added_product((early[0], early[1]), power, (late[0], late[1]))
    total = added_product((early[2] + late[2], early[3] + late[3]), (early[4], early[5]), (late[0], late[1]))
    reach = added_product((late[4], late[5]), power, (early[4], early[5]))
    for part, value in enumerate((carry, total, reach)):

        def store(block, value, part=part):
            for half in range(2):
                line = ((2 * block + half) * 3 + part) * PART
                packed_ref[line : line + PART] = value[half * PART : (half + 1) * PART]

        pack_slices(value[0], value[1], store)


def swap(value):
    return pltpu.roll(value, HALF, 1)


def factors(value, swapped):
    low = lane_low(value.shape)
    return jnp.where(low, value, swapped), jnp.where(low, -swapped, value)


def step(added, state, power):
    direct, cross = power
    here, there = state
    return added[0] + (here * direct + there * cross), added[1] + (there * direct - here * cross)


def squared(power):
    direct, cross = power
    return direct * direct - cross * cross, 2.0 * direct * cross


def core_of(where_ref):
    return lax.rem(where_ref[0], CORES)


def slice_values(ref, where_ref):
    modes, width = ref.shape
    chip, core = lax.rem(lax.div(where_ref[0], CORES), CHIPS_Z), core_of(where_ref)
    block, half = lax.div(chip, 2), lax.rem(chip, 2)
    chosen = jnp.zeros((PART, LANES), jnp.float32)
    for tile in range(width // LANES):
        for first in range(0, modes, PART):
            here = (lax.div(block, 2) == tile) & (core * SUB + half * PART == first)
            chosen = jnp.where(here, ref[first : first + PART, tile * LANES : (tile + 1) * LANES], chosen)
    chosen = jnp.where(lane_low(chosen.shape) == (lax.rem(block, 2) == 0), chosen, 0.0)
    return chosen + swap(chosen)


def span_power(span, decay_ref, angle_ref, where_ref):
    decay, angle = slice_values(decay_ref, where_ref), slice_values(angle_ref, where_ref)
    sine, cosine = sine_cosine(angle * float(span))
    radius = jnp.exp(-decay * float(span))
    return radius * cosine, jnp.where(lane_low(sine.shape), radius * sine, -radius * sine)


def lines_of(ref, place):
    return ref[place * PART : (place + 1) * PART]


def run_kernel(span, where_ref, own_ref, decay_ref, angle_ref, message_ref, inside_ref, power_ref):
    power = span_power(span, decay_ref, angle_ref, where_ref)
    power_ref[0:PART], power_ref[PART:] = power
    zero = jnp.zeros((PART, LANES), jnp.float32)
    state, total, reach = (zero, zero), zero, (zero, zero)
    reaches = []
    for z in range(CHIPS_Z):
        value = lines_of(own_ref, 3 * z + 2)
        reaches.append((value, swap(value)))
        reach = step(reaches[z], reach, power)
    for z in reversed(range(CHIPS_Z)):
        carry = lines_of(own_ref, 3 * z)
        inside_ref[z * PART : (z + 1) * PART] = state[0]
        direct, cross = factors(*reaches[z])
        total = total + (lines_of(own_ref, 3 * z + 1) + (state[0] * direct + state[1] * cross))
        state = step((carry, swap(carry)), state, power)
    for copy in range(message_ref.shape[0] // (3 * PART)):
        for part, value in enumerate((state[0], total, reach[0])):
            line = (3 * copy + part) * PART
            message_ref[line : line + PART] = value


def answer_kernel(where_ref, message_ref, inside_ref, power_ref, out_ref):
    mine = lax.div(where_ref[0], RUN)
    power = power_ref[0:PART], power_ref[PART:]
    run_power = power
    for _ in range(CHIPS_Z.bit_length() - 1):
        run_power = squared(run_power)
    zero = jnp.zeros((PART, LANES), jnp.float32)
    state, total = (zero, zero), zero
    entering = (zero, zero)
    for x in reversed(range(message_ref.shape[0] // (3 * PART))):
        carry, sums, reach = [lines_of(message_ref, 3 * x + part) for part in range(3)]
        entering = tuple(jnp.where(mine == x, new, old) for new, old in zip(state, entering))
        direct, cross = factors(reach, swap(reach))
        total = total + (sums + (state[0] * direct + state[1] * cross))
        state = step((carry, swap(carry)), state, run_power)
    for z in reversed(range(CHIPS_Z)):
        out_ref[2 * z * PART : (2 * z + 1) * PART] = lines_of(inside_ref, z) + entering[0]
        out_ref[(2 * z + 1) * PART : (2 * z + 2) * PART] = total
        entering = step((zero, zero), entering, power)


def residue_kernel(rows, where_ref, back_ref, keep_ref, got_ref, power_ref, mine_ref, send_ref, squares_ref):
    _, modes, width = mine_ref.shape
    first_core = core_of(where_ref) == 0
    power = shard_power(power_ref, rows)
    late = unpack_slices(slice_lines(back_ref, 0, 2), modes, width)
    carry = tuple(jnp.where(first_core, got_ref[part], keep_ref[part]) for part in range(2))
    early = added_product(carry, power, late)
    real, imaginary = unpack_slices(slice_lines(back_ref, 1, 2), modes, width)
    for part in range(2):
        mine_ref[part] = jnp.where(first_core, early[part], late[part])
        send_ref[part] = jnp.where(first_core, late[part], early[part])
    for ref in (mine_ref, send_ref):
        ref[2] = real
        ref[3] = -imaginary
    squares = jnp.sum(real * real + imaginary * imaginary, axis=0, keepdims=True)
    total = squares[:, 0:LANES]
    for tile in range(1, width // LANES):
        total = total + squares[:, tile * LANES : (tile + 1) * LANES]
    squares_ref[...] = jnp.broadcast_to(total, squares_ref.shape)


def both_halves(where_ref, mine_ref, other_ref, part):
    first_core = core_of(where_ref) == 0
    mine, other = mine_ref[part], other_ref[part]
    return jnp.concatenate([jnp.where(first_core, mine, other), jnp.where(first_core, other, mine)], axis=0)


def signal_kernel(
    where_ref, mine_ref, other_ref, weighted, my_chunks, other_chunks, my_powers, other_powers, decay_ref, key_ref,
    value_ref, residue_ref, skip_ref, grad_key_ref, grad_value_ref, signal,
):
    rows, width = weighted.shape
    scale = scale_of(decay_ref[...])
    first_core = core_of(where_ref) == 0
    weight = residue_ref[0] * scale, residue_ref[1] * scale
    chunk_refs, power_refs = (my_chunks, other_chunks), (my_powers, other_powers)
    weights = [tuple(chosen_half(first, part) for part in weight) for first in (first_core, core_of(where_ref) != 0)]
    place = lax.broadcasted_iota(jnp.int32, (SUB, width), 0)
    taps = []
    for lag in range(SUB):
        tap = None
        for half, powers in zip(weights, power_refs):
            part = half[0] * powers[2 * lag - 2] - half[1] * powers[2 * lag - 1] if lag else half[0]
            tap = part if tap is None else tap + part
        line = jnp.broadcast_to(jnp.sum(tap, axis=0, keepdims=True), (SUB, width))
        taps.append(jnp.where(place < SUB - lag, line, 0.0))
    taps[0] = taps[0] + skip_ref[...]
    begins = [product(half, (states[0], states[1])) for half, states in zip(weights, (mine_ref, other_ref))]
    span = 2 * LANES
    for column in range(0, width, span):
        cut = slice(column, column + span)
        scaled = [tuple(part[:, cut] for part in half) for half in weights]
        start = tuple(tuple(part[:, cut] for part in begin) for begin in begins)

        def block(i, states, cut=cut, scaled=scaled):
            j = rows // SUB - 1 - i
            for r in range(SUB):
                k = SUB - r
                total = None
                for powers, state in zip(power_refs, states):
                    part = powers[2 * k - 2, :, cut] * state[0] - powers[2 * k - 1, :, cut] * state[1]
                    total = part if total is None else total + part
                line = pl.ds(pl.multiple_of((j * SUB + r) * SUB, SUB), SUB)
                for part in range(span // LANES):
                    view = signal.at[cut.start // LANES + part]
                    view[line, :] = total[:, part * LANES : (part + 1) * LANES]
            after = []
            for powers, chunks, state, factor in zip(power_refs, chunk_refs, states, scaled):
                eighth = powers[2 * SUB - 2, :, cut], powers[2 * SUB - 1, :, cut]
                chunk = chunks[2 * j, :, cut], chunks[2 * j + 1, :, cut]
                after.append(added_product(product(factor, chunk), eighth, state))
            return tuple(after)

        lax.fori_loop(0, rows // SUB, block, start)
    pair = 2 * SUB
    for tile in range(width // LANES):
        cut = slice(tile * LANES, (tile + 1) * LANES)
        view = signal.at[tile]
        for first in range(0, rows, pair):
            parts = []
            for line in (first, first + SUB):
                w = weighted[line : line + SUB, cut]
                part = taps[0][:, cut] * w
                for lag in range(1, SUB):
                    part = part + taps[lag][:, cut] * pltpu.roll(w, SUB - lag, 0)
                for member in range(SUB):
                    part = part + view[pl.ds(line * SUB + member, SUB, stride=SUB), :]
                parts.append(part)
            part = jnp.concatenate(parts, axis=0)
            both = slice(first, first + pair)
            grad_key_ref[both, cut] = (part * value_ref[both, cut].astype(jnp.float32)).astype(jnp.bfloat16)
            grad_value_ref[both, cut] = (part * key_ref[both, cut].astype(jnp.float32)).astype(jnp.bfloat16)


def clip_kernel(clip_level, where_ref, squares_ref, mine_ref, other_ref, after_ref, out_ref):
    del after_ref
    norm = jnp.sqrt(jnp.sum(squares_ref[...], keepdims=True))
    factor = clip_level / jnp.maximum(norm, clip_level)
    for part in range(2):
        out_ref[part] = both_halves(where_ref, mine_ref, other_ref, 2 + part) * factor


def on_chip(*shape):
    return pltpu.VMEM(shape, jnp.float32)


def kept(array):
    return pltpu.with_memory_space_constraint(array, pltpu.VMEM)


def groups(shards):
    runs = shards // RUN
    along_z = [[x * RUN + z * CORES + c for z in range(CHIPS_Z)] for x in range(runs) for c in range(CORES)]
    along_x = [[x * RUN + inner for x in range(runs)] for inner in range(RUN)]
    return along_z, along_x


def on_device(
    grad_out, gate_query, key_input, value_input, decay_rate, pole_angle, residue, skip_gain
):
    rows, width = grad_out.shape
    modes = decay_rate.shape[0]
    shards, chan_shards = lax.axis_size(SEQ), lax.axis_size("chan")
    runs = shards // RUN
    along_z, along_x = groups(shards)
    flip = [(shard, shard ^ 1) for shard in range(shards)]
    where, grad_out = lax.optimization_barrier((lax.axis_index(SEQ).reshape(1), grad_out))
    scalar = pl.BlockSpec(memory_space=pltpu.SMEM)
    whole = pl.BlockSpec(memory_space=pltpu.VMEM)
    chunk_shape, power_shape = on_chip(2 * rows // SUB, SUB, width), on_chip(2 * SUB, SUB, width)
    send, other_chunks, other_powers, weighted, stored, lags, base, scale = pl.pallas_call(
        first_kernel,
        in_specs=[scalar] + [whole] * 6,
        out_shape=(
            on_chip(6, SUB, width),
            chunk_shape,
            power_shape,
            on_chip(rows, width),
            on_chip(rows, width),
            on_chip(SUB, SUB, width),
            on_chip(2, SUB, width),
            on_chip(SUB, width),
        ),
        name="first_half",
    )(where, grad_out, gate_query, key_input, value_input, decay_rate, pole_angle)
    got = kept(lax.ppermute(send, SEQ, flip))
    weighted = kept(weighted)
    keep, chunks, powers = pl.pallas_call(
        second_kernel,
        in_specs=[whole] * 5,
        out_shape=(on_chip(6, SUB, width), chunk_shape, power_shape),
        cost_estimate=pl.CostEstimate(flops=20 * rows * width * modes, bytes_accessed=12 * rows * width, transcendentals=0),
        name="second_half",
    )(weighted, kept(stored), kept(lags), kept(base), kept(scale))
    keep, powers = kept(keep), kept(powers)
    packed = pl.pallas_call(
        functools.partial(chip_kernel, rows),
        in_specs=[scalar] + [whole] * 3,
        out_shape=on_chip(3 * CHIPS_Z * PART, LANES),
        name="join_chip",
    )(where, keep, got, powers)
    own = kept(exchange(packed, CHIPS_Z, along_z))
    message, inside, power = pl.pallas_call(
        functools.partial(run_kernel, CORES * rows),
        in_specs=[scalar] + [whole] * 3,
        out_shape=(on_chip(3 * PART * runs, LANES), on_chip(CHIPS_Z * PART, LANES), on_chip(2 * PART, LANES)),
        name="join_run",
    )(where, own, kept(decay_rate), kept(pole_angle))
    message = kept(exchange(message, runs, along_x))
    answers = pl.pallas_call(
        answer_kernel,
        in_specs=[scalar] + [whole] * 3,
        out_shape=on_chip(2 * CHIPS_Z * PART, LANES),
        name="join_runs",
    )(where, message, kept(inside), kept(power))
    back = kept(exchange(answers, CHIPS_Z, along_z))
    mine, send, squares = pl.pallas_call(
        functools.partial(residue_kernel, rows),
        in_specs=[scalar] + [whole] * 4,
        out_shape=(
            on_chip(4, SUB, width),
            on_chip(4, SUB, width),
            on_chip(CORES * chan_shards, LANES),
        ),
        name="residue_sums",
    )(where, back, keep, got, powers)
    other = kept(lax.ppermute(send, SEQ, flip))
    mine = kept(mine)
    all_squares = kept(lax.all_to_all(squares, ("core", "chan"), 0, 0, tiled=True))
    grad_key, grad_value = pl.pallas_call(
        signal_kernel,
        in_specs=[scalar] + [whole] * 12,
        out_shape=(jax.ShapeDtypeStruct((rows, width), jnp.bfloat16),) * 2,
        scratch_shapes=[pltpu.VMEM((width // LANES, rows * SUB, LANES), jnp.float32)],
        cost_estimate=pl.CostEstimate(flops=20 * rows * width * modes, bytes_accessed=12 * rows * width, transcendentals=0),
        name="signal_pass",
    )(
        where, mine, other, weighted, kept(chunks), kept(other_chunks), powers, kept(other_powers), kept(decay_rate),
        kept(key_input), kept(value_input), kept(residue), skip_gain.reshape(1, width),
    )
    clip_level = math.sqrt(2 * modes * width * chan_shards)
    grad_residue = pl.pallas_call(
        functools.partial(clip_kernel, clip_level),
        in_specs=[scalar] + [whole] * 3 + [pl.BlockSpec(memory_space=pl.ANY)],
        out_shape=jax.ShapeDtypeStruct((2, modes, width), jnp.float32),
        name="clip",
    )(where, all_squares, mine, other, grad_key)
    return (grad_key, grad_value, grad_residue)


def exchange(array, members, over):
    sent = array.reshape(members, -1)
    return lax.all_to_all(sent, SEQ, 0, 0, tiled=True, axis_index_groups=over).reshape(array.shape)


def solution(mesh):
    shards, chan_shards = mesh.devices.shape
    split = Mesh(mesh.devices.reshape(shards // CORES, CORES, chan_shards), ("chip", "core", "chan"))
    return jax.shard_map(
        on_device,
        mesh=split,
        in_specs=(
            P(SEQ, "chan"),
            P(SEQ, "chan"),
            P(SEQ, "chan"),
            P(SEQ, "chan"),
            P(None, "chan"),
            P(None, "chan"),
            P(None, None, "chan"),
            P("chan"),
        ),
        out_specs=(P(SEQ, "chan"), P(SEQ, "chan"), P(None, None, "chan")),
        check_vma=False,
    )
```
